128 devices in a mesh: tok: 8 (over x, z_hi), feat: 16 (over y, z_lo, core).
Axes of the slice: x: 4, y: 4, z: 4 (z_hi: 2, z_lo: 2; z = z_hi * 2 + z_lo), core: 2. Of those that a mesh axis runs over, the one named last changes fastest.
Arguments:
- resid: bfloat16 [2048, 8192], P(None, ('tok', 'feat')), may hold values from -6 to 6
- resid_grad: bfloat16 [2048, 8192], P(None, ('tok', 'feat')), may hold values from -6 to 6
- active: int32 [16, 20], P('tok'), may hold values from 0 to 79, all different within a row
- w_enc: bfloat16 [8192, 10240], P(None, 'feat'), may hold values from -0.0625 to 0.0625
- b_enc: float32 [10240], P('feat'), may hold values from -3 to 3
- w_dec: bfloat16 [10240, 8192], P('feat'), may hold values from -0.25 to 0.25
- b_dec: float32 [8192], P('feat'), may hold values from -3 to 3
Outputs:
- feature_attr: float32 [2048, 10240], P('tok', 'feat')
- error: float32 [2048, 8192], P('tok', 'feat')
- error_attr: float32 [2048], P('tok')
The draws below stay inside these ranges and needn't reach their ends.
Inputs may be any that keep to these rules, and one draw needn't show every extreme that they name: `active`: each row lists 20 different feature blocks; every block is listed by some tile.
All inputs are finite; a program needn't handle non-finite values.
Results may differ from the reference program's by a relative error of at most 0.012.
Values may be sent and summed in bfloat16 or wider, within the bound.
A program may use at most 128 MiB of HBM per device.

```python
import jax
import jax.numpy as jnp
from jax import lax

D = 8192
BLOCK = 128
BLK_DEV = 5
TILE = 128
ACT = 20
TOKENS = 2048
NBLK = 80
NFEAT = 10240
TILES = 16
N_FEAT = 16


def with_spikes(array, stream_key, source, target, blocks, factor):
    def block_of(position):
        return (jnp.arange(array.shape[position]) // (array.shape[position] // blocks)).reshape((-1,) + (1,) * (array.ndim - 1 - position))

    near = jax.random.permutation(stream_key, blocks)[block_of(target)]
    other_side = (block_of(target) + blocks // 2) % blocks
    return jnp.where((block_of(source) == near) | (block_of(source) == other_side), factor * array, array)


def block_levels(own_key, extent, pieces, smallest, high):
    def one(axis_at, parts):
        heights = jax.random.uniform(jax.random.fold_in(jax.random.fold_in(own_key, 6), axis_at), (parts,), jnp.float32, smallest / len(pieces), high / len(pieces))
        return jnp.repeat(jnp.exp(heights), extent[axis_at] // parts).reshape((-1,) + (1,) * (len(extent) - axis_at - 1))

    loudness = one(*pieces[0])
    for cut in pieces[1:]:
        loudness = loudness * one(*cut)
    return loudness


def choose_distinct(key, rows, count, top, lift):
    ranking = jax.random.permutation(jax.random.fold_in(key, 1), count)
    boost = ranking
    for power in range(3):
        boost = boost * boost // count
    boost = boost * lift // count
    lots = jax.random.randint(jax.random.fold_in(key, 2), (rows, count), 0, 4096) + boost
    holders = jax.random.permutation(jax.random.fold_in(key, 3), rows)[jnp.arange(count) % rows]
    lots = jnp.where(jnp.arange(rows)[:, None] == holders[None, :], 1 << 14, lots)
    merit = lots * count + jnp.arange(count)
    return lax.top_k(merit.astype(jnp.int32), top)[1].astype(jnp.int32)


def noise(own_key, extent, deviation, reach, cuts=(), kind=jnp.bfloat16):
    values = jax.random.normal(own_key, extent, jnp.float32) * deviation
    if len(cuts) > 0:
        values = block_levels(own_key, extent, cuts, -0.22, 0.18) * values
    return jnp.clip(values, min=-reach, max=reach).astype(kind)


def gaussian_with(rng, extent, spread, bound, shards, heavy, kind=jnp.bfloat16):
    array = spread * jax.random.normal(rng, extent, jnp.float32)
    if shards:
        array = array * block_levels(rng, extent, shards, -0.22, 0.18)
    return jnp.clip(with_spikes(array, jax.random.fold_in(rng, 3), *heavy), -bound, bound).astype(kind)


def setup_inputs(seed: int = 0) -> dict:
    key_of = jax.random.split(jax.random.key(seed), 8)
    resid = noise(key_of[0], (TOKENS, D), 1.0, 6.0, ((1, 128),))
    resid_grad = noise(key_of[1], (TOKENS, D), 1.0, 6.0, ((1, 128),))
    active = choose_distinct(key_of[2], TILES, NBLK, ACT, 4096)
    w_enc = noise(key_of[3], (D, NFEAT), D ** -0.5, 0.0625, ((1, 16),))
    b_enc = noise(key_of[4], (NFEAT,), 0.5, 3.0, ((0, 16),), jnp.float32)
    w_dec = gaussian_with(key_of[5], (NFEAT, D), (ACT * BLOCK // 2) ** -0.5, 0.25, ((0, 16),), (0, 1, 16, 2.0))
    b_dec = noise(key_of[6], (D,), 0.5, 3.0, ((0, 16),), jnp.float32)
    return dict(resid=resid, resid_grad=resid_grad, active=active, w_enc=w_enc, b_enc=b_enc, w_dec=w_dec, b_dec=b_dec)


def reference(resid, resid_grad, active, w_enc, b_enc, w_dec, b_dec):
    pre = jnp.dot(resid, w_enc, preferred_element_type=jnp.float32) + b_enc
    block_ids = jnp.arange(NBLK, dtype=jnp.int32)
    hits = jnp.any(active[:, :, None] == block_ids[None, None, :], axis=1).astype(jnp.float32)
    shaped = jnp.maximum(pre, 0.0).reshape(TILES, TILE, NBLK, BLOCK) * hits[:, None, :, None]
    acts = shaped.reshape(TOKENS, NFEAT).astype(jnp.bfloat16)
    group = BLK_DEV * BLOCK
    acts_groups = jnp.transpose(acts.reshape(TOKENS, N_FEAT, group), (1, 0, 2))
    dec_groups = w_dec.reshape(N_FEAT, group, D)

    def add_group(total, pair):
        part = jnp.dot(pair[0], pair[1], preferred_element_type=jnp.float32).astype(jnp.bfloat16)
        return total + part.astype(jnp.float32), None

    summed, _ = lax.scan(add_group, jnp.zeros((TOKENS, D), jnp.float32), (acts_groups, dec_groups))
    recon = summed + b_dec
    error = resid.astype(jnp.float32) - recon
    error_attr = jnp.sum(error * resid_grad.astype(jnp.float32), axis=1)
    proj = lax.dot_general(resid_grad, w_dec, (((1,), (1,)), ((), ())), preferred_element_type=jnp.float32)
    feature_attr = acts.astype(jnp.float32) * proj
    return feature_attr, error, error_attr
```

```python
import jax
import jax.numpy as jnp
from jax import lax
from jax.sharding import PartitionSpec as P

BLOCK = 128
TILE = 128


def gather_rows(part):
    n_tok = lax.axis_size("tok")
    total, width = part.shape
    own = part.T.reshape(width, n_tok, total // n_tok).transpose(1, 0, 2)
    own = lax.all_to_all(own, "tok", split_axis=0, concat_axis=0, tiled=True)
    cols = lax.all_gather(own, "feat", axis=1, tiled=False)
    return cols.reshape(-1, total // n_tok)


def per_device(resid, resid_grad, active, w_enc, b_enc, w_dec, b_dec):
    rows_x = gather_rows(resid)
    rows_g = gather_rows(resid_grad)
    tok_rows = rows_x.shape[1]
    feat_dev = w_enc.shape[1]
    blocks = feat_dev // BLOCK
    tiles_dev = active.shape[0]
    block_ids = lax.axis_index("feat") * blocks + jnp.arange(blocks, dtype=jnp.int32)
    hits = jnp.any(active[:, :, None] == block_ids[None, None, :], axis=1).astype(jnp.float32)
    pre = lax.dot_general(rows_x, w_enc, (((0,), (0,)), ((), ())), preferred_element_type=jnp.float32) + b_enc
    shaped = jnp.maximum(pre, 0.0).reshape(tiles_dev, TILE, blocks, BLOCK) * hits[:, None, :, None]
    acts = shaped.reshape(tok_rows, feat_dev).astype(jnp.bfloat16)
    partial_recon = jnp.dot(acts, w_dec, preferred_element_type=jnp.float32)
    recon_share = lax.psum_scatter(
        partial_recon.astype(jnp.bfloat16), "feat", scatter_dimension=1, tiled=True
    ).astype(jnp.float32)
    share = recon_share.shape[1]
    start = lax.axis_index("feat") * share
    own_x = lax.dynamic_slice_in_dim(rows_x, start, share, 0).T
    own_g = lax.dynamic_slice_in_dim(rows_g, start, share, 0).T
    recon = recon_share + b_dec
    error = own_x.astype(jnp.float32) - recon
    local_terms = jnp.sum(error * own_g.astype(jnp.float32), axis=1)
    error_attr = lax.psum(local_terms, "feat")
    proj = lax.dot_general(
        rows_g, w_dec, (((0,), (1,)), ((), ())), preferred_element_type=jnp.float32
    )
    feature_attr = acts.astype(jnp.float32) * proj
    return (feature_attr, error, error_attr)


def solution(mesh):
    placed = (
        P(None, ("tok", "feat")),
        P(None, ("tok", "feat")),
        P("tok", None),
        P(None, "feat"),
        P("feat"),
        P("feat", None),
        P("feat"),
    )
    return jax.shard_map(
        per_device,
        mesh=mesh,
        in_specs=placed,
        out_specs=(P("tok", "feat"), P("tok", "feat"), P("tok")),
        check_vma=False,
    )
```

```python
import functools

import jax
import jax.numpy as jnp
from jax import lax
from jax.experimental import pallas as pl
from jax.experimental.pallas import tpu as pltpu
from jax.sharding import PartitionSpec as P

MESH = pl.DeviceIdType.MESH
F32, BF16 = jnp.float32, jnp.bfloat16
NX, NY = 4, 4
ROWS = 256
FD = 640
NSEM = 220


class Copies:
    def __init__(self, send, recv):
        self.send, self.recv, self.n, self.open = send, recv, 0, []

    def new(self, src, dst, dev):
        k = self.n
        self.n += 1
        return pltpu.make_async_remote_copy(
            src_ref=src, dst_ref=dst, send_sem=self.send.at[k], recv_sem=self.recv.at[k],
            device_id=dev, device_id_type=MESH,
        ), k

    def start(self, src, dst, dev):
        copy, k = self.new(src, dst, dev)
        copy.start()
        self.open.append(copy)
        return k

    def arrived(self, k, mine, dev):
        pltpu.make_async_remote_copy(
            src_ref=mine, dst_ref=mine, send_sem=self.send.at[k], recv_sem=self.recv.at[k],
            device_id=dev, device_id_type=MESH,
        ).wait_recv()

    def drain(self):
        for copy in self.open:
            copy.wait_send()


def kernel(xt, gt, active, wenc_h, benc, wdec_h, bdec, fa_h, err_h, attr_h,
           X, G, wenc, wdec, pre, acts, projt, part, r0, r1, ra, rb, red, reu, rz, errb, fab, sums, got,
           attr, local_sem, send, recv, tsend, trecv):
    tok, feat = lax.axis_index("tok"), lax.axis_index("feat")
    x, zh = tok // 2, tok % 2
    y, z, c = feat // 4, (feat // 2) % 2, feat % 2
    p = feat // 2
    up, dn, opp = (y + 1) % NY, (y + 3) % NY, (y + 2) % NY

    def at(yy, zz, cc):
        return {"tok": tok, "feat": yy * 4 + zz * 2 + cc}

    d_core, d_z, d_up, d_dn = at(y, z, 1 - c), at(y, 1 - z, c), at(up, z, c), at(dn, z, c)

    w1 = pltpu.make_async_copy(wenc_h, wenc, local_sem.at[0])
    w2 = pltpu.make_async_copy(wdec_h, wdec, local_sem.at[1])
    own = []
    for i, (src, dst) in enumerate(((xt, X), (gt, G))):
        own.append(pltpu.make_async_copy(
            src.at[:, pl.ds(pl.multiple_of(tok * ROWS, ROWS), ROWS)], dst.at[p, 0, x, c], local_sem.at[2 + i]))
        own[i].start()
    w1.start()
    w2.start()

    def tok_peer(dx, other):
        xx = (x + dx) % NX
        zz = 1 - zh if other else zh
        return xx * 2 + zz, (y * 2 + (1 - z if other else z)) * 2 + c

    peers = [(dx, o) for o in (0, 1) for dx in range(NX) if dx or o]
    barrier = pltpu.get_barrier_semaphore()
    for dx, o in peers:
        tt, ff = tok_peer(dx, o)
        pl.semaphore_signal(barrier, inc=1, device_id={"tok": tt, "feat": ff}, device_id_type=MESH)
    for dev in (d_core, d_z, d_up, d_dn):
        pl.semaphore_signal(barrier, inc=1, device_id=dev, device_id_type=MESH)
    pl.semaphore_wait(barrier, len(peers) + 4)

    tcopies = []
    for i, (src, dst) in enumerate(((xt, X), (gt, G))):
        for dx, o in ((2, 0), (2, 1), (1, 0), (3, 0), (1, 1), (3, 1), (0, 1)):
            tt, ff = tok_peer(dx, o)
            k = i * 8 + o * 4 + dx
            copy = pltpu.make_async_remote_copy(
                src_ref=src.at[:, pl.ds(pl.multiple_of(tt * ROWS, ROWS), ROWS)],
                dst_ref=dst.at[ff // 2, o, x, c],
                send_sem=tsend.at[k], recv_sem=trecv.at[k],
                device_id={"tok": tt, "feat": ff}, device_id_type=MESH)
            copy.start()
            tcopies.append(copy)

    def tok_arrived(i, dst, o):
        for dx in range(NX):
            if dx or o:
                tt, ff = tok_peer((NX - dx) % NX, o)
                slab = dst.at[p, o, (x + NX - dx) % NX, c]
                k = i * 8 + o * 4 + dx
                pltpu.make_async_remote_copy(
                    src_ref=slab, dst_ref=slab, send_sem=tsend.at[k], recv_sem=trecv.at[k],
                    device_id={"tok": tt, "feat": ff}, device_id_type=MESH).wait_recv()

    cp = Copies(send, recv)

    def blk(buf, yy, zz, s, cc, half=None):
        if half is None:
            return buf.at[yy * 2 + zz, s, :, cc]
        return buf.at[yy * 2 + zz, s, pl.ds(half * 2, 2), cc]

    class Gather:
        def __init__(self, buf):
            self.buf, self.core, self.k = buf, {}, {}

        def send(self, name, yy, zz, s, dev, half=None):
            b = blk(self.buf, yy, zz, s, c, half)
            self.k[name] = cp.start(b, b, dev)

        def wait(self, name, yy, zz, s, dev, half=None):
            cp.arrived(self.k[name], blk(self.buf, yy, zz, s, c, half), dev)

        def to_core(self, name, yy, zz, s):
            b = blk(self.buf, yy, zz, s, c)
            self.core[name] = (cp.start(b, b, d_core), yy, zz, s)

        def from_core(self, name):
            k, yy, zz, s = self.core[name]
            cp.arrived(k, blk(self.buf, yy, zz, s, 1 - c), d_core)

    def gather(buf, step, head):
        g = Gather(buf)
        zo = 1 - z

        def ready(name, yy, zz, s):
            g.from_core(name)
            step(yy, zz, s)

        head(0)
        g.send("z0", y, z, 0, d_z)
        g.send("u0", y, z, 0, d_up)
        g.send("d0", y, z, 0, d_dn)
        g.to_core("o0", y, z, 0)
        head(1)
        g.send("u1", y, z, 1, d_up)
        g.send("d1", y, z, 1, d_dn)
        g.send("z1", y, z, 1, d_z)
        g.to_core("o1", y, z, 1)
        ready("o0", y, z, 0)
        g.wait("z0", y, zo, 0, d_z)
        g.send("uz", y, zo, 0, d_up)
        g.send("dz", y, zo, 0, d_dn)
        g.to_core("p0", y, zo, 0)
        g.wait("u0", dn, z, 0, d_dn)
        g.wait("d0", up, z, 0, d_up)
        g.to_core("u0c", dn, z, 0)
        g.to_core("d0c", up, z, 0)
        ready("o1", y, z, 1)
        ready("p0", y, zo, 0)
        g.wait("u1", dn, z, 1, d_dn)
        g.send("fu1", dn, z, 1, d_up, 0)
        g.send("zu1", dn, z, 1, d_z)
        g.wait("d1", up, z, 1, d_up)
        g.send("fd1", up, z, 1, d_dn, 1)
        g.send("zd1", up, z, 1, d_z)
        g.send("fu0", dn, z, 0, d_up, 0)
        g.send("fd0", up, z, 0, d_dn, 1)
        g.to_core("u1c", dn, z, 1)
        g.to_core("d1c", up, z, 1)
        g.wait("z1", y, zo, 1, d_z)
        g.to_core("p1", y, zo, 1)
        ready("u0c", dn, z, 0)
        ready("d0c", up, z, 0)
        g.wait("uz", dn, zo, 0, d_dn)
        g.send("fuz", dn, zo, 0, d_up, 0)
        g.wait("dz", up, zo, 0, d_up)
        g.send("fdz", up, zo, 0, d_dn, 1)
        g.to_core("uzc", dn, zo, 0)
        g.to_core("dzc", up, zo, 0)
        g.wait("fu1", opp, z, 1, d_dn, 0)
        g.wait("fd1", opp, z, 1, d_up, 1)
        g.send("zo1", opp, z, 1, d_z)
        g.to_core("op1", opp, z, 1)
        ready("u1c", dn, z, 1)
        ready("d1c", up, z, 1)
        ready("p1", y, zo, 1)
        g.wait("zu1", dn, zo, 1, d_z)
        g.to_core("zu1c", dn, zo, 1)
        g.wait("fu0", opp, z, 0, d_dn, 0)
        g.wait("fd0", opp, z, 0, d_up, 1)
        g.to_core("op0", opp, z, 0)
        ready("uzc", dn, zo, 0)
        ready("dzc", up, zo, 0)
        ready("op1", opp, z, 1)
        g.wait("fuz", opp, zo, 0, d_dn, 0)
        g.wait("fdz", opp, zo, 0, d_up, 1)
        g.to_core("opz", opp, zo, 0)
        g.wait("zd1", up, zo, 1, d_z)
        g.to_core("zd1c", up, zo, 1)
        ready("zu1c", dn, zo, 1)
        ready("op0", opp, z, 0)
        ready("opz", opp, zo, 0)
        ready("zd1c", up, zo, 1)
        g.wait("zo1", opp, zo, 1, d_z)
        g.to_core("zo1c", opp, zo, 1)
        ready("zo1c", opp, zo, 1)

    def place(yy, zz, s):
        if s == 0:
            return zh, yy * 2 + zz
        return 1 - zh, yy * 2 + 1 - zz

    pre[...] = jnp.zeros_like(pre)

    def pre_step(yy, zz, s):
        zp, q = place(yy, zz, s)
        lhs = X[yy * 2 + zz, s].reshape(512, ROWS)
        rhs = wenc[:, zp, q].reshape(512, FD)
        pre[...] += lax.dot_general(lhs, rhs, (((0,), (0,)), ((), ())), preferred_element_type=F32)

    def head_x(s):
        if s == 0:
            own[0].wait()
        tok_arrived(0, X, s)
        if s == 1:
            w1.wait()

    gather(X, pre_step, head_x)

    lane_block = feat * 5 + lax.broadcasted_iota(jnp.int32, (1, FD), 1) // 128
    for tile in range(2):
        hit = jnp.zeros((1, FD), F32)
        for j in range(active.shape[1]):
            hit = jnp.where(lane_block == active[tile, j], 1.0, hit)
        rows = pl.ds(tile * 128, 128)
        acts[rows, :] = (jnp.maximum(pre[rows, :] + benc[...].reshape(1, FD), 0.0) * hit).astype(BF16)

    w2.wait()

    @pl.loop(0, 16)
    def _(i):
        q = (i % 8) * 2 + jnp.where(i < 8, 1 - c, c)
        cols = pl.ds(pl.multiple_of(q * 512, 512), 512)
        part[q] = jnp.dot(acts[...], wdec[:, cols], preferred_element_type=F32).astype(BF16)

    core_k = [cp.start(part.at[q * 2 + 1 - c], r0.at[q], d_core) for q in range(8)]

    projt[...] = jnp.zeros_like(projt)

    def proj_step(yy, zz, s):
        zp, q = place(yy, zz, s)
        lhs = jnp.concatenate(
            [wdec[:, pl.ds(pl.multiple_of((xx * 2 + zp) * 1024 + q * 128, 128), 128)] for xx in range(NX)], axis=1)
        projt[...] += jnp.dot(lhs, G[yy * 2 + zz, s].reshape(512, ROWS), preferred_element_type=F32)

    def head_g(s):
        if s == 0:
            own[1].wait()
        tok_arrived(1, G, s)

    gather(G, proj_step, head_g)

    ox, oz = feat // 4, (feat // 2) % 2
    os = jnp.where(oz == zh, 0, 1)
    term = jnp.zeros((ROWS, 128), F32)
    bd = bdec[...].reshape(1, 512)
    for j in range(4):
        q = (feat % 2) * 4 + j
        pb = q + os * (1 - 2 * (q % 2))
        xs = X[pb, os, ox].reshape(128, ROWS).astype(F32).T - bd[:, j * 128:(j + 1) * 128]
        gs = G[pb, os, ox].reshape(128, ROWS).astype(F32).T
        errb[:, j * 128:(j + 1) * 128] = xs
        term = term + xs * gs
    for j in range(5):
        lanes = slice(j * 128, (j + 1) * 128)
        f = acts[:, lanes].astype(F32) * projt[lanes, :].T
        fab[:, lanes] = f
        term = term - f
    out1 = pltpu.make_async_copy(fab, fa_h, local_sem.at[4])
    out1.start()
    sums[0] = jnp.broadcast_to(jnp.sum(term.T, axis=0, keepdims=True), (8, ROWS))

    def pair(i, dev):
        k = cp.start(sums.at[i], got.at[i], dev)
        return lambda: cp.arrived(k, got.at[i], dev)

    def add(dst, *srcs):
        total = dst[...].astype(F32)
        for s in srcs:
            total = total + s[...].astype(F32)
        dst[...] = total.astype(BF16)

    w_pair = pair(0, d_core)
    for q in range(8):
        cp.arrived(core_k[q], r0.at[q], d_core)

    @pl.loop(0, 8)
    def _(q):
        add(part.at[q * 2 + c], r0.at[q])

    def unit(u, yy, lo, n):
        zz = (z, 1 - z, z)[u]
        return part.at[(yy * 2 + zz) * 2 + c, pl.ds((0, 128, 128)[u] + lo, n)]

    zk = [cp.start(part.at[(yy * 2 + 1 - z) * 2 + c, pl.ds(0, 128)], r1.at[yy], d_z) for yy in range(NY)]
    ka, kb, ku, kd = {}, {}, {}, {}

    def first(u):
        ka[u] = cp.start(unit(u, opp, 0, 64), ra.at[u], d_up)
        kb[u] = cp.start(unit(u, opp, 64, 64), rb.at[u], d_dn)

    def second(u):
        cp.arrived(ka[u], ra.at[u], d_dn)
        add(unit(u, up, 0, 64), ra.at[u])
        ku[u] = cp.start(unit(u, up, 0, 128), red.at[u], d_up)
        cp.arrived(kb[u], rb.at[u], d_up)
        add(unit(u, dn, 64, 64), rb.at[u])
        kd[u] = cp.start(unit(u, dn, 0, 128), reu.at[u], d_dn)

    first(1)
    first(2)
    w_pair()
    sums[1] = sums[0] + got[0]
    w_pair = pair(1, d_z)
    second(1)
    for yy in range(NY):
        cp.arrived(zk[yy], r1.at[yy], d_z)

    @pl.loop(0, NY)
    def _(yy):
        add(part.at[(yy * 2 + z) * 2 + c, pl.ds(0, 128)], r1.at[yy])

    first(0)
    w_pair()
    sums[2] = sums[1] + got[1]
    d_even = at(y + 1 - 2 * (y % 2), z, c)
    d_odd = at(3 - y, z, c)
    w_pair = pair(2, d_even)
    second(2)
    cp.arrived(ku[1], red.at[1], d_dn)
    cp.arrived(kd[1], reu.at[1], d_up)
    add(unit(1, y, 0, 128), red.at[1], reu.at[1])
    k_last = cp.start(unit(1, y, 0, 128), rz, d_z)
    w_pair()
    sums[3] = sums[2] + got[2]
    w_pair = pair(3, d_odd)
    second(0)
    w_pair()
    attr[...] = (sums[3] + got[3])[0:1, :]
    out2 = pltpu.make_async_copy(attr, attr_h, local_sem.at[5])
    out2.start()

    cp.arrived(ku[2], red.at[2], d_dn)
    cp.arrived(kd[2], reu.at[2], d_up)
    cp.arrived(k_last, rz, d_z)
    hi = pl.ds(128, 128)
    errb[hi, :] = errb[hi, :] - (unit(2, y, 0, 128)[...].astype(F32) + red[2].astype(F32) + reu[2].astype(F32)
                                 + rz[...].astype(F32))
    out3 = pltpu.make_async_copy(errb.at[hi], err_h.at[hi], local_sem.at[6])
    out3.start()
    cp.arrived(ku[0], red.at[0], d_dn)
    cp.arrived(kd[0], reu.at[0], d_up)
    lo = pl.ds(0, 128)
    errb[lo, :] = errb[lo, :] - (unit(0, y, 0, 128)[...].astype(F32) + red[0].astype(F32) + reu[0].astype(F32))
    out4 = pltpu.make_async_copy(errb.at[lo], err_h.at[lo], local_sem.at[7])
    out4.start()
    for copy in tcopies:
        copy.wait_send()
    cp.drain()
    for o in (out1, out2, out3, out4):
        o.wait()


def per_device(resid, resid_grad, active, w_enc, b_enc, w_dec, b_dec):
    any_, vmem = pl.BlockSpec(memory_space=pl.ANY), pl.BlockSpec(memory_space=pltpu.VMEM)
    V = pltpu.VMEM
    fa, err, attr = pl.pallas_call(
        kernel,
        out_shape=(
            jax.ShapeDtypeStruct((ROWS, FD), F32),
            jax.ShapeDtypeStruct((ROWS, 512), F32),
            jax.ShapeDtypeStruct((1, ROWS), F32),
        ),
        in_specs=[any_, any_, pl.BlockSpec(memory_space=pltpu.SMEM), any_, vmem, any_, vmem],
        out_specs=(any_, any_, any_),
        scratch_shapes=[
            V((8, 2, NX, 2, 64, ROWS), BF16),
            V((8, 2, NX, 2, 64, ROWS), BF16),
            V((NX, 2, 8, 128, FD), BF16),
            V((FD, 8192), BF16),
            V((ROWS, FD), F32),
            V((ROWS, FD), BF16),
            V((FD, ROWS), F32),
            V((16, ROWS, 512), BF16),
            V((8, ROWS, 512), BF16),
            V((NY, 128, 512), BF16),
            V((3, 64, 512), BF16),
            V((3, 64, 512), BF16),
            V((3, 128, 512), BF16),
            V((3, 128, 512), BF16),
            V((128, 512), BF16),
            V((ROWS, 512), F32),
            V((ROWS, FD), F32),
            V((4, 8, ROWS), F32),
            V((4, 8, ROWS), F32),
            V((1, ROWS), F32),
            pltpu.SemaphoreType.DMA((8,)),
            pltpu.SemaphoreType.DMA((NSEM,)),
            pltpu.SemaphoreType.DMA((NSEM,)),
            pltpu.SemaphoreType.DMA((16,)),
            pltpu.SemaphoreType.DMA((16,)),
        ],
        compiler_params=pltpu.CompilerParams(
            collective_id=0, has_side_effects=True, vmem_limit_bytes=60 * 1024 * 1024),
    )(resid.T, resid_grad.T, active, w_enc.reshape(NX, 2, 8, 128, FD), b_enc, w_dec, b_dec)
    return fa, err, attr.reshape(ROWS)


def solution(mesh):
    placed = (
        P(None, ("tok", "feat")),
        P(None, ("tok", "feat")),
        P("tok", None),
        P(None, "feat"),
        P("feat"),
        P("feat", None),
        P("feat"),
    )
    return jax.shard_map(
        per_device,
        mesh=mesh,
        in_specs=placed,
        out_specs=(P("tok", "feat"), P("tok", "feat"), P("tok")),
        check_vma=False,
    )
```

```python
import contextlib
import math

import jax
import jax.numpy as jnp
from jax import lax
from jax.experimental import pallas as pl
from jax.experimental.pallas import tpu as pltpu
from jax.sharding import PartitionSpec as P

MESH = pl.DeviceIdType.MESH
F32, BF16 = jnp.float32, jnp.bfloat16
NX, NY = 4, 4
ROWS = 256
FD = 640
NRECV = 90
SCOPED = False


def mark(name):
    return jax.named_scope(name) if SCOPED else contextlib.nullcontext()


class Copies:
    def __init__(self, send, recv):
        self.send, self.recv, self.keys, self.sent = send, recv, {}, {}

    def start(self, key, src, dst, dev, group=0):
        k = self.keys.setdefault(key, len(self.keys))
        pltpu.make_async_remote_copy(
            src_ref=src, dst_ref=dst, send_sem=self.send.at[group], recv_sem=self.recv.at[k],
            device_id=dev, device_id_type=MESH,
        ).start()
        self.sent[group] = self.sent.get(group, 0) + math.prod(src.shape) * src.dtype.itemsize

    def arrived(self, key, mine, dev):
        with mark(f"w{key}"):
            pltpu.make_async_remote_copy(
                src_ref=mine, dst_ref=mine, send_sem=self.send.at[0], recv_sem=self.recv.at[self.keys[key]],
                device_id=dev, device_id_type=MESH,
            ).wait_recv()

    def drain(self, group, rows, row_bytes, dev):
        count, rest = divmod(self.sent[group], row_bytes)
        assert rest == 0
        mine = rows(count)
        pltpu.make_async_remote_copy(
            src_ref=mine, dst_ref=mine, send_sem=self.send.at[group], recv_sem=self.recv.at[0],
            device_id=dev, device_id_type=MESH,
        ).wait_send()


def kernel(xt, gt, active, wenc_h, benc, wdec_h, bdec, fab, errb, attr,
           X, G, wenc, wdec, wpeer, pre, acts, apeer, projt, part, r1, ra, rb, red, reu, rz, sums, got,
           local_sem, send, recv):
    tok, feat = lax.axis_index("tok"), lax.axis_index("feat")
    x, zh = tok // 2, tok % 2
    y, z, c = feat // 4, (feat // 2) % 2, feat % 2
    p = feat // 2
    up, dn, opp = (y + 1) % NY, (y + 3) % NY, (y + 2) % NY

    def at(yy, zz, cc):
        return {"tok": tok, "feat": yy * 4 + zz * 2 + cc}

    d_core, d_z, d_up, d_dn = at(y, z, 1 - c), at(y, 1 - z, c), at(up, z, c), at(dn, z, c)

    w1 = pltpu.make_async_copy(wenc_h, wenc, local_sem.at[0])
    w2 = pltpu.make_async_copy(wdec_h, wdec, local_sem.at[1])
    own = []
    for i, (src, dst) in enumerate(((xt, X), (gt, G))):
        own.append(pltpu.make_async_copy(
            src.at[:, pl.ds(pl.multiple_of(tok * ROWS, ROWS), ROWS)], dst.at[p, 0, x, c], local_sem.at[2 + i]))
        own[i].start()
    w1.start()
    w2.start()

    def tok_peer(dx, other):
        xx = (x + dx) % NX
        zz = 1 - zh if other else zh
        return xx * 2 + zz, (y * 2 + (1 - z if other else z)) * 2 + c

    peers = [(dx, o) for o in (0, 1) for dx in range(NX) if dx or o]
    barrier = pltpu.get_barrier_semaphore()
    for dx, o in peers:
        tt, ff = tok_peer(dx, o)
        pl.semaphore_signal(barrier, inc=1, device_id={"tok": tt, "feat": ff}, device_id_type=MESH)
    d_diag, d_opp = at(y, 1 - z, 1 - c), at(opp, z, c)
    group = (d_core, d_z, d_up, d_dn, d_diag, d_opp)
    for dev in group:
        pl.semaphore_signal(barrier, inc=1, device_id=dev, device_id_type=MESH)
    with mark("barrier"):
        pl.semaphore_wait(barrier, len(peers) + len(group))

    cp = Copies(send, recv)
    for i, (src, dst) in enumerate(((xt, X), (gt, G))):
        for dx, o in ((2, 0), (2, 1), (1, 0), (3, 0), (1, 1), (3, 1), (0, 1)):
            tt, ff = tok_peer(dx, o)
            cp.start(f"t{o}{dx}" if i == 0 else "tg",
                     src.at[:, pl.ds(pl.multiple_of(tt * ROWS, ROWS), ROWS)], dst.at[ff // 2, o, x, c],
                     {"tok": tt, "feat": ff}, 1)

    sent_wpeer = []

    def send_wpeer():
        q = len(sent_wpeer)
        sent_wpeer.append(q)
        cols = pl.ds(pl.multiple_of((q * 2 + 1 - c) * 512, 512), 512)
        cp.start(f"wpeer{q // 4}", wdec_h.at[:, cols], wpeer.at[q], d_core)

    def blk(buf, yy, zz, s, cc, part=None):
        if part is None:
            return buf.at[yy * 2 + zz, s, :, cc]
        return buf.at[yy * 2 + zz, s, part, cc]

    zo = 1 - z
    halves = (pl.ds(0, 2), pl.ds(2, 2))

    class Gather:
        def __init__(self, tag, buf, step):
            self.tag, self.buf, self.step, self.core = tag, buf, step, {}
            self.group = 0 if tag == "x" else 4

        def send(self, name, yy, zz, s, dev, part=None):
            b = blk(self.buf, yy, zz, s, c, part)
            cp.start(self.tag + name, b, b, dev, self.group)

        def wait(self, name, yy, zz, s, dev):
            cp.arrived(self.tag + name, blk(self.buf, yy, zz, s, c), dev)

        def to_core(self, name, yy, zz, s, part=None):
            b = blk(self.buf, yy, zz, s, c, part)
            cp.start(self.tag + name + "c", b, b, d_core, self.group)
            self.core[name] = (yy, zz, s)

        def steps(self, *names):
            for name in names:
                yy, zz, s = self.core[name]
                cp.arrived(self.tag + name + "c", blk(self.buf, yy, zz, s, 1 - c), d_core)
                with mark(f"s{self.tag}{name}"):
                    self.step(yy, zz, s)

        def begin(self):
            self.send("u1", y, z, 1, d_up)
            self.send("d1", y, z, 1, d_dn)
            self.send("z0", y, z, 0, d_z)
            self.send("u0", y, z, 0, d_up)
            self.send("d0", y, z, 0, d_dn)
            self.send("z1", y, z, 1, d_z)
            self.to_core("o0", y, z, 0)
            self.to_core("o1", y, z, 1)

        def begin_slab(self, s, xx):
            self.send(f"u{s}", y, z, s, d_up, xx)
            self.send(f"d{s}", y, z, s, d_dn, xx)
            self.send(f"z{s}", y, z, s, d_z, xx)
            self.to_core(f"o{s}", y, z, s, xx)

        def a(self):
            self.wait("u1", dn, z, 1, d_dn)
            self.send("zu1", dn, z, 1, d_z)
            self.send("f1", dn, z, 1, d_up, halves[0])
            self.wait("d1", up, z, 1, d_up)
            self.send("zd1", up, z, 1, d_z)
            self.send("f1", up, z, 1, d_dn, halves[1])

        def b(self):
            self.wait("z0", y, zo, 0, d_z)
            self.send("uz", y, zo, 0, d_up)
            self.send("dz", y, zo, 0, d_dn)
            self.to_core("p0", y, zo, 0)

        def c(self):
            self.wait("u0", dn, z, 0, d_dn)
            self.send("f0", dn, z, 0, d_up, halves[0])
            self.wait("d0", up, z, 0, d_up)
            self.send("f0", up, z, 0, d_dn, halves[1])
            self.to_core("u0c", dn, z, 0)
            self.to_core("d0c", up, z, 0)
            self.to_core("u1c", dn, z, 1)
            self.to_core("d1c", up, z, 1)

        def c1(self):
            self.wait("z1", y, zo, 1, d_z)
            self.to_core("p1", y, zo, 1)

        def d(self):
            self.wait("f1", opp, z, 1, d_dn)
            self.send("zo1", opp, z, 1, d_z)
            self.to_core("op1", opp, z, 1)

        def e(self):
            self.wait("uz", dn, zo, 0, d_dn)
            self.send("fz", dn, zo, 0, d_up, halves[0])
            self.wait("dz", up, zo, 0, d_up)
            self.send("fz", up, zo, 0, d_dn, halves[1])
            self.to_core("uzc", dn, zo, 0)
            self.to_core("dzc", up, zo, 0)

        def f(self):
            self.wait("f0", opp, z, 0, d_dn)
            self.to_core("op0", opp, z, 0)

        def g(self):
            self.wait("zu1", dn, zo, 1, d_z)
            self.to_core("zu1c", dn, zo, 1)
            self.wait("zd1", up, zo, 1, d_z)
            self.to_core("zd1c", up, zo, 1)

        def h(self):
            self.wait("fz", opp, zo, 0, d_dn)
            self.to_core("opz", opp, zo, 0)

        def i(self):
            self.wait("zo1", opp, zo, 1, d_z)
            self.to_core("zo1c", opp, zo, 1)

    def place(yy, zz, s):
        if s == 0:
            return zh, yy * 2 + zz
        return 1 - zh, yy * 2 + 1 - zz

    pre[...] = jnp.zeros_like(pre)
    projt[...] = jnp.zeros_like(projt)

    def pre_step(yy, zz, s):
        zp, q = place(yy, zz, s)
        lhs = X[yy * 2 + zz, s].reshape(512, ROWS)
        rhs = wenc[:, zp, q].reshape(512, FD)
        pre[...] += lax.dot_general(lhs, rhs, (((0,), (0,)), ((), ())), preferred_element_type=F32)

    def proj_step(yy, zz, s):
        zp, q = place(yy, zz, s)
        lhs = jnp.concatenate(
            [wdec[:, pl.ds(pl.multiple_of((xx * 2 + zp) * 1024 + q * 128, 128), 128)] for xx in range(NX)], axis=1)
        projt[...] += jnp.dot(lhs, G[yy * 2 + zz, s].reshape(512, ROWS), preferred_element_type=F32)

    gx = Gather("x", X, pre_step)
    gg = Gather("g", G, proj_step)
    for o, dx in ((0, 0), (0, 1), (0, 3), (1, 0), (1, 1), (1, 3), (0, 2), (1, 2)):
        if dx or o:
            cp.arrived(f"t{o}{dx}", X.at[p, o, (x + NX - dx) % NX, c], d_z)
        else:
            own[0].wait()
        gx.begin_slab(o, (x + NX - dx) % NX)
    send_wpeer()
    gx.a()
    gx.b()
    send_wpeer()
    gx.c()
    send_wpeer()
    with mark("w1"):
        w1.wait()
    gx.steps("o0")
    gx.c1()
    send_wpeer()
    gx.d()
    send_wpeer()
    gx.steps("o1")
    gx.e()
    send_wpeer()
    own[1].wait()
    cp.arrived("tg", G.at[pl.ds(0, 7), 0, 0, 0], d_z)
    gg.begin()
    gx.steps("p0", "u0c", "d0c")
    gx.f()
    send_wpeer()
    gx.steps("u1c", "d1c", "p1")
    gx.g()
    send_wpeer()
    gx.h()
    gx.steps("uzc", "dzc", "op1", "op0", "zu1c", "opz")
    gx.i()
    gx.steps("zd1c", "zo1c")

    with mark("acts"):
        lane_block = feat * 5 + lax.broadcasted_iota(jnp.int32, (1, FD), 1) // 128
        for tile in range(2):
            hit = jnp.zeros((1, FD), F32)
            for j in range(active.shape[1]):
                hit = jnp.where(lane_block == active[tile, j], 1.0, hit)
            rows = pl.ds(tile * 128, 128)
            acts[rows, :] = (jnp.maximum(pre[rows, :] + benc[...].reshape(1, FD), 0.0) * hit).astype(BF16)
    cp.start("acts", acts, apeer, d_core, 2)
    with mark("w2"):
        w2.wait()

    def share(q):
        cols = pl.ds(pl.multiple_of((q * 2 + c) * 512, 512), 512)
        lhs = jnp.concatenate([acts[...], apeer[...]], axis=1)
        rhs = jnp.concatenate([wdec[:, cols], wpeer[q]], axis=0)
        part[q] = jnp.dot(lhs, rhs, preferred_element_type=F32).astype(BF16)

    def add(dst, *srcs):
        total = dst[...].astype(F32)
        for s in srcs:
            total = total + s[...].astype(F32)
        dst[...] = total.astype(BF16)

    def unit(u, yy, lo, n):
        zz = (z, zo, z)[u]
        return part.at[yy * 2 + zz, pl.ds((0, 128, 128)[u] + lo, n)]

    def first(u):
        cp.start(f"a{u}", unit(u, opp, 0, 64), ra.at[u], d_up, 4)
        cp.start(f"b{u}", unit(u, opp, 64, 64), rb.at[u], d_dn, 4)

    def second(u):
        cp.arrived(f"a{u}", ra.at[u], d_dn)
        add(unit(u, up, 0, 64), ra.at[u])
        cp.start(f"u{u}", unit(u, up, 0, 128), red.at[u], d_up, 4)
        cp.arrived(f"b{u}", rb.at[u], d_up)
        add(unit(u, dn, 64, 64), rb.at[u])
        cp.start(f"d{u}", unit(u, dn, 0, 128), reu.at[u], d_dn, 4)

    def third(u):
        cp.arrived(f"u{u}", red.at[u], d_dn)
        cp.arrived(f"d{u}", reu.at[u], d_up)

    rel = (opp, up, dn, y)

    def zsend(i):
        cp.start(f"z{i}", part.at[rel[i] * 2 + zo, pl.ds(0, 128)], r1.at[i], d_z, 4)

    def zadd(i):
        cp.arrived(f"z{i}", r1.at[i], d_z)
        add(part.at[rel[i] * 2 + z, pl.ds(0, 128)], r1.at[i])

    gg.steps("o0")
    gg.a()
    gg.b()
    cp.arrived("acts", apeer, d_core)
    cp.arrived("wpeer0", wpeer.at[pl.ds(0, 4)], d_core)
    cp.arrived("wpeer1", wpeer.at[pl.ds(4, 4)], d_core)
    with mark("share_a"):
        @pl.loop(0, NY)
        def _(i):
            share(((y + 2 + i) % NY) * 2 + zo)
    gg.c()
    gg.d()
    zsend(0)
    first(1)
    with mark("share_b"):
        @pl.loop(0, NY)
        def _(i):
            share(((y + 2 + i) % NY) * 2 + z)
    gg.e()
    first(2)
    for i in range(1, NY):
        zsend(i)
    gg.c1()
    gg.steps("o1", "p0")
    gg.f()
    gg.steps("u0c")
    gg.g()
    gg.h()
    gg.steps("d0c", "u1c")
    second(1)
    gg.steps("d1c", "p1", "uzc", "dzc", "op0", "op1", "zu1c", "zd1c")
    gg.i()
    gg.steps("opz")
    second(2)
    gg.steps("zo1c")
    with mark("err"):
        ox, oz = feat // 4, (feat // 2) % 2
        os = jnp.where(oz == zh, 0, 1)
        term = jnp.zeros((ROWS, 128), F32)
        bd = bdec[...].reshape(1, 512)
        for j in range(4):
            q = (feat % 2) * 4 + j
            pb = q + os * (1 - 2 * (q % 2))
            xs = X[pb, os, ox].reshape(128, ROWS).astype(F32).T - bd[:, j * 128:(j + 1) * 128]
            gs = G[pb, os, ox].reshape(128, ROWS).astype(F32).T
            errb[:, j * 128:(j + 1) * 128] = xs
            term = term + xs * gs
        for j in range(5):
            lanes = slice(j * 128, (j + 1) * 128)
            f = acts[:, lanes].astype(F32) * projt[lanes, :].T
            fab[:, lanes] = f
            term = term - f
        sums[0] = jnp.broadcast_to(jnp.sum(term.T, axis=0, keepdims=True), (8, ROWS))

    def exchange(key, src, slots, mine, devs):
        slots[mine] = src[...]
        for dev in devs:
            cp.start(key, src, slots.at[mine], dev, 3)

    def total(key, slots):
        cp.arrived(key, slots.at[pl.ds(0, 3)], d_z)
        return slots[0] + slots[1] + slots[2] + slots[3]

    exchange("s0", sums.at[0], got.at[0], z * 2 + c, (d_core, d_z, d_diag))
    zadd(0)
    first(0)
    third(1)
    add(unit(1, y, 0, 128), red.at[1], reu.at[1])
    cp.start("last", unit(1, y, 0, 128), rz, d_z, 4)
    sums[1] = total("s0", got.at[0])
    exchange("s1", sums.at[1], got.at[1], y, (d_up, d_dn, d_opp))
    zadd(1)
    zadd(2)
    second(0)
    third(2)
    zadd(3)
    attr[...] = total("s1", got.at[1])[0:1, :]
    third(0)
    lo = pl.ds(0, 128)
    errb[lo, :] = errb[lo, :] - (unit(0, y, 0, 128)[...].astype(F32) + red[0].astype(F32) + reu[0].astype(F32))
    cp.arrived("last", rz, d_z)
    hi = pl.ds(128, 128)
    errb[hi, :] = errb[hi, :] - (unit(2, y, 0, 128)[...].astype(F32) + red[2].astype(F32) + reu[2].astype(F32)
                                 + rz[...].astype(F32))
    with mark("drain"):
        assert len(cp.keys) == NRECV, len(cp.keys)
        cp.drain(0, lambda n: wdec.at[pl.ds(0, n)], 8192 * 2, d_z)
        cp.drain(4, lambda n: wdec.at[pl.ds(0, n)], 8192 * 2, d_z)
        cp.drain(1, lambda n: X.at[pl.ds(0, n), 0, 0], 65536, d_z)
        cp.drain(2, lambda n: acts, ROWS * FD * 2, d_z)
        cp.drain(3, lambda n: part.at[0, pl.ds(0, n)], 1024, d_z)


def per_device(resid, resid_grad, active, w_enc, b_enc, w_dec, b_dec):
    any_, vmem = pl.BlockSpec(memory_space=pl.ANY), pl.BlockSpec(memory_space=pltpu.VMEM)
    V = pltpu.VMEM
    outs = [((ROWS, FD), F32), ((ROWS, 512), F32), ((1, ROWS), F32)]
    held = pl.pallas_call(
        kernel,
        out_shape=tuple(V(*o) for o in outs),
        in_specs=[any_, any_, pl.BlockSpec(memory_space=pltpu.SMEM), any_, vmem, any_, vmem],
        out_specs=(vmem, vmem, vmem),
        scratch_shapes=[
            V((8, 2, NX, 2, 64, ROWS), BF16),
            V((8, 2, NX, 2, 64, ROWS), BF16),
            V((NX, 2, 8, 128, FD), BF16),
            V((FD, 8192), BF16),
            V((8, FD, 512), BF16),
            V((ROWS, FD), F32),
            V((ROWS, FD), BF16),
            V((ROWS, FD), BF16),
            V((FD, ROWS), F32),
            V((8, ROWS, 512), BF16),
            V((NY, 128, 512), BF16),
            V((3, 64, 512), BF16),
            V((3, 64, 512), BF16),
            V((3, 128, 512), BF16),
            V((3, 128, 512), BF16),
            V((128, 512), BF16),
            V((2, 8, ROWS), F32),
            V((2, 4, 8, ROWS), F32),
            pltpu.SemaphoreType.DMA((4,)),
            pltpu.SemaphoreType.DMA((5,)),
            pltpu.SemaphoreType.DMA((NRECV,)),
        ],
        compiler_params=pltpu.CompilerParams(
            collective_id=0, has_side_effects=True, vmem_limit_bytes=58 * 1024 * 1024),
    )(resid.T, resid_grad.T, active, w_enc.reshape(NX, 2, 8, 128, FD), b_enc, w_dec, b_dec)
    fa, err, attr = held
    return fa, err, attr.reshape(ROWS)


def solution(mesh):
    placed = (
        P(None, ("tok", "feat")),
        P(None, ("tok", "feat")),
        P("tok", None),
        P(None, "feat"),
        P("feat"),
        P("feat", None),
        P("feat"),
    )
    return jax.shard_map(
        per_device,
        mesh=mesh,
        in_specs=placed,
        out_specs=(P("tok", "feat"), P("tok", "feat"), P("tok")),
        check_vma=False,
    )
```

```python
import contextlib
import math

import jax
import jax.numpy as jnp
from jax import lax
from jax.experimental import pallas as pl
from jax.experimental.pallas import tpu as pltpu
from jax.sharding import PartitionSpec as P

MESH = pl.DeviceIdType.MESH
F32, BF16 = jnp.float32, jnp.bfloat16
NX, NY = 4, 4
ROWS = 256
FD = 640
NRECV = 90
N1, N2 = 96, 160
SCOPED = False


def mark(name):
    return jax.named_scope(name) if SCOPED else contextlib.nullcontext()


class Copies:
    def __init__(self, send, recv):
        self.send, self.recv, self.keys, self.sent = send, recv, {}, {}

    def start(self, key, src, dst, dev, group=0):
        k = self.keys.setdefault(key, len(self.keys))
        pltpu.make_async_remote_copy(
            src_ref=src, dst_ref=dst, send_sem=self.send.at[group], recv_sem=self.recv.at[k],
            device_id=dev, device_id_type=MESH,
        ).start()
        self.sent[group] = self.sent.get(group, 0) + math.prod(src.shape) * src.dtype.itemsize

    def arrived(self, key, mine, dev):
        with mark(f"w{key}"):
            pltpu.make_async_remote_copy(
                src_ref=mine, dst_ref=mine, send_sem=self.send.at[0], recv_sem=self.recv.at[self.keys[key]],
                device_id=dev, device_id_type=MESH,
            ).wait_recv()

    def drain(self, group, rows, row_bytes, dev):
        count, rest = divmod(self.sent[group], row_bytes)
        assert rest == 0
        mine = rows(count)
        pltpu.make_async_remote_copy(
            src_ref=mine, dst_ref=mine, send_sem=self.send.at[group], recv_sem=self.recv.at[0],
            device_id=dev, device_id_type=MESH,
        ).wait_send()


def kernel(xt, gt, active_h, wenc_h, benc_h, wdec_h, bdec_h, fab, errb, attr,
           active, benc, bdec,
           X, G, wenc, wdec, wpeer, pre, acts, apeer, projt, part, r1, ra, rb, red, reu, rz, sums, got,
           local_sem, send, recv):
    tok, feat = lax.axis_index("tok"), lax.axis_index("feat")
    x, zh = tok // 2, tok % 2
    y, z, c = feat // 4, (feat // 2) % 2, feat % 2
    p = feat // 2
    up, dn, opp = (y + 1) % NY, (y + 3) % NY, (y + 2) % NY

    def at(yy, zz, cc):
        return {"tok": tok, "feat": yy * 4 + zz * 2 + cc}

    d_core, d_z, d_up, d_dn = at(y, z, 1 - c), at(y, 1 - z, c), at(up, z, c), at(dn, z, c)

    def tok_peer(dx, other):
        xx = (x + dx) % NX
        zz = 1 - zh if other else zh
        return xx * 2 + zz, (y * 2 + (1 - z if other else z)) * 2 + c

    peers = [(dx, o) for o in (0, 1) for dx in range(NX) if dx or o]
    barrier = pltpu.get_barrier_semaphore()
    for dx, o in peers:
        tt, ff = tok_peer(dx, o)
        pl.semaphore_signal(barrier, inc=1, device_id={"tok": tt, "feat": ff}, device_id_type=MESH)
    d_diag, d_opp = at(y, 1 - z, 1 - c), at(opp, z, c)
    group = (d_core, d_z, d_up, d_dn, d_diag, d_opp)
    for dev in group:
        pl.semaphore_signal(barrier, inc=1, device_id=dev, device_id_type=MESH)
    small = [pltpu.make_async_copy(s, d, local_sem.at[4 + i])
             for i, (s, d) in enumerate(((active_h, active), (benc_h, benc), (bdec_h, bdec)))]
    w1 = pltpu.make_async_copy(wenc_h, wenc, local_sem.at[0])
    w2 = pltpu.make_async_copy(wdec_h, wdec, local_sem.at[1])
    own = []
    for i, (src, dst) in enumerate(((xt, X), (gt, G))):
        own.append(pltpu.make_async_copy(
            src.at[:, pl.ds(pl.multiple_of(tok * ROWS, ROWS), ROWS)], dst.at[p, 0, x, c], local_sem.at[2 + i]))
        own[i].start()
    w1.start()
    for copy in small:
        copy.start()
    w2.start()

    with mark("barrier"):
        pl.semaphore_wait(barrier, len(peers) + len(group))

    cp = Copies(send, recv)
    for i, (src, dst) in enumerate(((xt, X), (gt, G))):
        for dx, o in ((1, 0), (3, 0), (0, 1), (1, 1), (3, 1), (2, 0), (2, 1)):
            tt, ff = tok_peer(dx, o)
            cp.start(f"t{o}{dx}" if i == 0 else "tg",
                     src.at[:, pl.ds(pl.multiple_of(tt * ROWS, ROWS), ROWS)], dst.at[ff // 2, o, x, c],
                     {"tok": tt, "feat": ff}, 1)

    sent_wpeer = []

    def send_wpeer():
        q = len(sent_wpeer)
        sent_wpeer.append(q)
        cols = pl.ds(pl.multiple_of((q * 2 + 1 - c) * 512, 512), 512)
        cp.start(f"wpeer{q // 4}", wdec_h.at[:, cols], wpeer.at[q], d_core)

    def blk(buf, yy, zz, s, cc, part=None):
        if part is None:
            return buf.at[yy * 2 + zz, s, :, cc]
        return buf.at[yy * 2 + zz, s, part, cc]

    zo = 1 - z
    halves = (pl.ds(0, 2), pl.ds(2, 2))

    class Gather:
        def __init__(self, tag, buf, step):
            self.tag, self.buf, self.step, self.core = tag, buf, step, {}
            self.group = 0 if tag == "x" else 4

        def send(self, name, yy, zz, s, dev, part=None):
            b = blk(self.buf, yy, zz, s, c, part)
            cp.start(self.tag + name, b, b, dev, self.group)

        def wait(self, name, yy, zz, s, dev):
            cp.arrived(self.tag + name, blk(self.buf, yy, zz, s, c), dev)

        def to_core(self, name, yy, zz, s, part=None):
            b = blk(self.buf, yy, zz, s, c, part)
            cp.start(self.tag + name + "c", b, b, d_core, self.group)
            self.core[name] = (yy, zz, s)

        def steps(self, *names):
            for name in names:
                yy, zz, s = self.core[name]
                cp.arrived(self.tag + name + "c", blk(self.buf, yy, zz, s, 1 - c), d_core)
                with mark(f"s{self.tag}{name}"):
                    self.step(yy, zz, s)

        def begin(self):
            self.send("u1", y, z, 1, d_up)
            self.send("d1", y, z, 1, d_dn)
            for dx in (1, 2, 3):
                self.begin_slab(0, (x + NX - dx) % NX)
            self.send("z1", y, z, 1, d_z)
            self.to_core("o1", y, z, 1)

        def begin_slab(self, s, xx):
            self.send(f"u{s}", y, z, s, d_up, xx)
            self.send(f"d{s}", y, z, s, d_dn, xx)
            self.send(f"z{s}", y, z, s, d_z, xx)
            self.to_core(f"o{s}", y, z, s, xx)

        def a(self):
            self.wait("u1", dn, z, 1, d_dn)
            self.send("zu1", dn, z, 1, d_z)
            self.send("f1", dn, z, 1, d_up, halves[0])
            self.wait("d1", up, z, 1, d_up)
            self.send("zd1", up, z, 1, d_z)
            self.send("f1", up, z, 1, d_dn, halves[1])

        def b(self):
            self.wait("z0", y, zo, 0, d_z)
            self.send("uz", y, zo, 0, d_up)
            self.send("dz", y, zo, 0, d_dn)
            self.to_core("p0", y, zo, 0)

        def c(self):
            self.wait("u0", dn, z, 0, d_dn)
            self.send("f0", dn, z, 0, d_up, halves[0])
            self.wait("d0", up, z, 0, d_up)
            self.send("f0", up, z, 0, d_dn, halves[1])
            self.to_core("u0c", dn, z, 0)
            self.to_core("d0c", up, z, 0)
            self.to_core("u1c", dn, z, 1)
            self.to_core("d1c", up, z, 1)

        def c1(self):
            self.wait("z1", y, zo, 1, d_z)
            self.to_core("p1", y, zo, 1)

        def d(self):
            self.wait("f1", opp, z, 1, d_dn)
            self.send("zo1", opp, z, 1, d_z)
            self.to_core("op1", opp, z, 1)

        def e(self):
            self.wait("uz", dn, zo, 0, d_dn)
            self.send("fz", dn, zo, 0, d_up, halves[0])
            self.wait("dz", up, zo, 0, d_up)
            self.send("fz", up, zo, 0, d_dn, halves[1])
            self.to_core("uzc", dn, zo, 0)
            self.to_core("dzc", up, zo, 0)

        def f(self):
            self.wait("f0", opp, z, 0, d_dn)
            self.to_core("op0", opp, z, 0)

        def g(self):
            self.wait("zu1", dn, zo, 1, d_z)
            self.to_core("zu1c", dn, zo, 1)
            self.wait("zd1", up, zo, 1, d_z)
            self.to_core("zd1c", up, zo, 1)

        def h(self):
            self.wait("fz", opp, zo, 0, d_dn)
            self.to_core("opz", opp, zo, 0)

        def i(self):
            self.wait("zo1", opp, zo, 1, d_z)
            self.to_core("zo1c", opp, zo, 1)

    def place(yy, zz, s):
        if s == 0:
            return zh, yy * 2 + zz
        return 1 - zh, yy * 2 + 1 - zz

    pre[...] = jnp.zeros_like(pre)
    projt[...] = jnp.zeros_like(projt)

    def pre_step(yy, zz, s):
        zp, q = place(yy, zz, s)
        lhs = X[yy * 2 + zz, s].reshape(512, ROWS)
        rhs = wenc[:, zp, q].reshape(512, FD)
        pre[...] += lax.dot_general(lhs, rhs, (((0,), (0,)), ((), ())), preferred_element_type=F32)

    def proj_step(yy, zz, s):
        zp, q = place(yy, zz, s)
        lhs = jnp.concatenate(
            [wdec[:, pl.ds(pl.multiple_of((xx * 2 + zp) * 1024 + q * 128, 128), 128)] for xx in range(NX)], axis=1)
        projt[...] += jnp.dot(lhs, G[yy * 2 + zz, s].reshape(512, ROWS), preferred_element_type=F32)

    gx = Gather("x", X, pre_step)
    gg = Gather("g", G, proj_step)
    for o, dx in ((0, 0), (0, 1), (0, 3), (1, 0), (1, 1), (1, 3), (0, 2), (1, 2)):
        if dx or o:
            cp.arrived(f"t{o}{dx}", X.at[p, o, (x + NX - dx) % NX, c], d_z)
        else:
            own[0].wait()
        gx.begin_slab(o, (x + NX - dx) % NX)
        if dx == 0 and o == 0:
            own[1].wait()
            gg.begin_slab(0, x)
        if (o, dx) in ((0, 0), (0, 1), (1, 0)):
            send_wpeer()
    send_wpeer()
    gx.a()
    gx.b()
    gx.c()
    send_wpeer()
    with mark("w1"):
        w1.wait()
        for copy in small:
            copy.wait()
    gx.steps("o0", "o1")
    gx.c1()
    send_wpeer()
    gx.steps("p0", "u0c")
    gx.d()
    send_wpeer()
    gx.steps("d0c", "u1c", "d1c", "p1")
    gx.e()
    cp.arrived("tg", G.at[pl.ds(0, 7), 0, 0, 0], d_z)
    gg.begin()
    send_wpeer()
    gx.f()
    gx.g()
    gx.steps("op1", "uzc", "dzc", "op0")
    gx.h()
    gx.i()
    gx.steps("zu1c", "zd1c", "opz")
    gg.a()
    gx.steps("zo1c")

    with mark("acts"):
        lane_block = feat * 5 + lax.broadcasted_iota(jnp.int32, (1, FD), 1) // 128
        for tile in range(2):
            hit = jnp.zeros((1, FD), F32)
            for j in range(active.shape[1]):
                hit = jnp.where(lane_block == active[tile, j], 1.0, hit)
            rows = pl.ds(tile * 128, 128)
            acts[rows, :] = (jnp.maximum(pre[rows, :] + benc[...].reshape(1, FD), 0.0) * hit).astype(BF16)
    cp.start("acts", acts, apeer, d_core, 2)
    with mark("w2"):
        w2.wait()

    def share(q):
        cols = pl.ds(pl.multiple_of((q * 2 + c) * 512, 512), 512)
        lhs = jnp.concatenate([acts[...], apeer[...]], axis=1)
        rhs = jnp.concatenate([wdec[:, cols], wpeer[q]], axis=0)
        part[q] = jnp.dot(lhs, rhs, preferred_element_type=F32).astype(BF16)

    def add(dst, *srcs):
        total = dst[...].astype(F32)
        for s in srcs:
            total = total + s[...].astype(F32)
        dst[...] = total.astype(BF16)

    def unit(u, yy, lo, n):
        zz = (z, zo, z)[u]
        return part.at[yy * 2 + zz, pl.ds((0, N1, N1)[u] + lo, n)]

    rows_of, cut = (N1, N2, N2), (48, 80, 80)

    def land(buf, u, n):
        return buf.at[u, pl.ds(0, n)]

    def first(u):
        a, b = cut[u], rows_of[u] - cut[u]
        cp.start(f"a{u}", unit(u, opp, 0, a), land(ra, u, a), d_up, 4)
        cp.start(f"b{u}", unit(u, opp, a, b), land(rb, u, b), d_dn, 4)

    def second(u):
        n, a, b = rows_of[u], cut[u], rows_of[u] - cut[u]
        cp.arrived(f"a{u}", land(ra, u, a), d_dn)
        add(unit(u, up, 0, a), land(ra, u, a))
        cp.start(f"u{u}", unit(u, up, 0, n), land(red, u, n), d_up, 4)
        cp.arrived(f"b{u}", land(rb, u, b), d_up)
        add(unit(u, dn, a, b), land(rb, u, b))
        cp.start(f"d{u}", unit(u, dn, 0, n), land(reu, u, n), d_dn, 4)

    def third(u):
        cp.arrived(f"u{u}", land(red, u, rows_of[u]), d_dn)
        cp.arrived(f"d{u}", land(reu, u, rows_of[u]), d_up)

    rel = (opp, up, dn, y)

    def zsend(i):
        cp.start(f"z{i}", part.at[rel[i] * 2 + zo, pl.ds(0, N1)], r1.at[i], d_z, 4)

    def zadd(i):
        cp.arrived(f"z{i}", r1.at[i], d_z)
        add(part.at[rel[i] * 2 + z, pl.ds(0, N1)], r1.at[i])

    gg.b()
    gg.steps("o0", "o1")
    cp.arrived("acts", apeer, d_core)
    cp.arrived("wpeer0", wpeer.at[pl.ds(0, 4)], d_core)
    cp.arrived("wpeer1", wpeer.at[pl.ds(4, 4)], d_core)
    with mark("share_a"):
        @pl.loop(0, NY)
        def _(i):
            share(((y + 2 + i) % NY) * 2 + zo)
    gg.c()
    gg.d()
    first(1)
    gg.c1()
    with mark("share_b"):
        @pl.loop(0, NY)
        def _(i):
            share(((y + 2 + i) % NY) * 2 + z)
    gg.e()
    zsend(0)
    zsend(1)
    first(2)
    gg.steps("p0", "u0c")
    gg.f()
    gg.steps("d0c", "u1c")
    second(1)
    gg.g()
    gg.steps("d1c", "p1")
    gg.h()
    gg.steps("uzc", "dzc", "op0", "op1")
    gg.i()
    zsend(2)
    gg.steps("zu1c", "zd1c", "opz")
    second(2)
    gg.steps("zo1c")
    with mark("err"):
        ox, oz = feat // 4, (feat // 2) % 2
        os = jnp.where(oz == zh, 0, 1)
        term = jnp.zeros((ROWS, 128), F32)
        bd = bdec[...].reshape(1, 512)
        for j in range(4):
            q = (feat % 2) * 4 + j
            pb = q + os * (1 - 2 * (q % 2))
            xs = X[pb, os, ox].reshape(128, ROWS).astype(F32).T - bd[:, j * 128:(j + 1) * 128]
            gs = G[pb, os, ox].reshape(128, ROWS).astype(F32).T
            errb[:, j * 128:(j + 1) * 128] = xs
            term = term + xs * gs
        for j in range(5):
            lanes = slice(j * 128, (j + 1) * 128)
            f = acts[:, lanes].astype(F32) * projt[lanes, :].T
            fab[:, lanes] = f
            term = term - f
        sums[0] = jnp.broadcast_to(jnp.sum(term.T, axis=0, keepdims=True), (8, ROWS))

    def exchange(key, src, slots, mine, devs):
        slots[mine] = src[...]
        for dev in devs:
            cp.start(key, src, slots.at[mine], dev, 3)

    def total(key, slots):
        cp.arrived(key, slots.at[pl.ds(0, 3)], d_z)
        return slots[0] + slots[1] + slots[2] + slots[3]

    exchange("s0", sums.at[0], got.at[0], z * 2 + c, (d_core, d_z, d_diag))
    zsend(3)
    zadd(0)
    first(0)
    third(1)
    add(unit(1, y, 0, N2), red.at[1], reu.at[1])
    cp.start("last", unit(1, y, 0, N2), rz, d_z, 4)
    zadd(1)
    sums[1] = total("s0", got.at[0])
    exchange("s1", sums.at[1], got.at[1], y, (d_up, d_dn, d_opp))
    zadd(2)
    second(0)
    third(2)
    zadd(3)
    attr[...] = total("s1", got.at[1])[0:1, :]
    third(0)
    lo, hi = pl.ds(0, N1), pl.ds(N1, N2)
    errb[lo, :] = errb[lo, :] - (unit(0, y, 0, N1)[...].astype(F32) + red[0, lo].astype(F32) + reu[0, lo].astype(F32))
    cp.arrived("last", rz, d_z)
    errb[hi, :] = errb[hi, :] - (unit(2, y, 0, N2)[...].astype(F32) + red[2].astype(F32) + reu[2].astype(F32)
                                 + rz[...].astype(F32))
    with mark("drain"):
        assert len(cp.keys) == NRECV, len(cp.keys)
        cp.drain(0, lambda n: wdec.at[pl.ds(0, n)], 8192 * 2, d_z)
        cp.drain(4, lambda n: wdec.at[pl.ds(0, n)], 8192 * 2, d_z)
        cp.drain(1, lambda n: X.at[pl.ds(0, n), 0, 0], 65536, d_z)
        cp.drain(2, lambda n: acts, ROWS * FD * 2, d_z)
        cp.drain(3, lambda n: part.at[0, pl.ds(0, n)], 1024, d_z)


def write_out(fa, err, attr, fa_h, err_h, attr_h, sem):
    copies = [pltpu.make_async_copy(s, d, sem.at[i])
              for i, (s, d) in enumerate(((fa, fa_h), (err, err_h), (attr, attr_h)))]
    for copy in copies:
        copy.start()
    for copy in copies:
        copy.wait()


def per_device(resid, resid_grad, active, w_enc, b_enc, w_dec, b_dec):
    any_, vmem = pl.BlockSpec(memory_space=pl.ANY), pl.BlockSpec(memory_space=pltpu.VMEM)
    V = pltpu.VMEM
    outs = [((ROWS, FD), F32), ((ROWS, 512), F32), ((1, ROWS), F32)]
    held = pl.pallas_call(
        kernel,
        out_shape=tuple(V(*o) for o in outs),
        in_specs=[any_] * 7,
        out_specs=(vmem, vmem, vmem),
        scratch_shapes=[
            pltpu.SMEM(active.shape, active.dtype),
            V(b_enc.shape, F32),
            V(b_dec.shape, F32),
            V((8, 2, NX, 2, 64, ROWS), BF16),
            V((8, 2, NX, 2, 64, ROWS), BF16),
            V((NX, 2, 8, 128, FD), BF16),
            V((FD, 8192), BF16),
            V((8, FD, 512), BF16),
            V((ROWS, FD), F32),
            V((ROWS, FD), BF16),
            V((ROWS, FD), BF16),
            V((FD, ROWS), F32),
            V((8, ROWS, 512), BF16),
            V((NY, N1, 512), BF16),
            V((3, 80, 512), BF16),
            V((3, 80, 512), BF16),
            V((3, N2, 512), BF16),
            V((3, N2, 512), BF16),
            V((N2, 512), BF16),
            V((2, 8, ROWS), F32),
            V((2, 4, 8, ROWS), F32),
            pltpu.SemaphoreType.DMA((7,)),
            pltpu.SemaphoreType.DMA((5,)),
            pltpu.SemaphoreType.DMA((NRECV,)),
        ],
        compiler_params=pltpu.CompilerParams(
            collective_id=0, has_side_effects=True, vmem_limit_bytes=58 * 1024 * 1024),
    )(resid.T, resid_grad.T, active, w_enc.reshape(NX, 2, 8, 128, FD), b_enc, w_dec, b_dec)
    fa, err, attr = pl.pallas_call(
        write_out,
        out_shape=tuple(jax.ShapeDtypeStruct(*o) for o in outs),
        in_specs=[vmem] * 3,
        out_specs=(any_,) * 3,
        scratch_shapes=[pltpu.SemaphoreType.DMA((3,))],
    )(*(pltpu.with_memory_space_constraint(h, pltpu.VMEM) for h in held))
    return fa, err, attr.reshape(ROWS)


def solution(mesh):
    placed = (
        P(None, ("tok", "feat")),
        P(None, ("tok", "feat")),
        P("tok", None),
        P(None, "feat"),
        P("feat"),
        P("feat", None),
        P("feat"),
    )
    return jax.shard_map(
        per_device,
        mesh=mesh,
        in_specs=placed,
        out_specs=(P("tok", "feat"), P("tok", "feat"), P("tok")),
        check_vma=False,
    )
```

```python
import contextlib
import math

import jax
import jax.numpy as jnp
from jax import lax
from jax.experimental import pallas as pl
from jax.experimental.pallas import tpu as pltpu
from jax.sharding import PartitionSpec as P

MESH = pl.DeviceIdType.MESH
F32, BF16 = jnp.float32, jnp.bfloat16
NX, NY = 4, 4
ROWS = 256
FD = 640
NRECV = 92
N1, N2 = 96, 160
SCOPED = False


def mark(name):
    return jax.named_scope(name) if SCOPED else contextlib.nullcontext()


class Copies:
    def __init__(self, send, recv):
        self.send, self.recv, self.keys, self.sent = send, recv, {}, {}

    def start(self, key, src, dst, dev, group=0):
        k = self.keys.setdefault(key, len(self.keys))
        pltpu.make_async_remote_copy(
            src_ref=src, dst_ref=dst, send_sem=self.send.at[group], recv_sem=self.recv.at[k],
            device_id=dev, device_id_type=MESH,
        ).start()
        self.sent[group] = self.sent.get(group, 0) + math.prod(src.shape) * src.dtype.itemsize

    def arrived(self, key, mine, dev):
        with mark(f"w{key}"):
            pltpu.make_async_remote_copy(
                src_ref=mine, dst_ref=mine, send_sem=self.send.at[0], recv_sem=self.recv.at[self.keys[key]],
                device_id=dev, device_id_type=MESH,
            ).wait_recv()

    def drain(self, group, rows, row_bytes, dev):
        count, rest = divmod(self.sent[group], row_bytes)
        assert rest == 0
        mine = rows(count)
        pltpu.make_async_remote_copy(
            src_ref=mine, dst_ref=mine, send_sem=self.send.at[group], recv_sem=self.recv.at[0],
            device_id=dev, device_id_type=MESH,
        ).wait_send()


def kernel(xt, gt, active_h, wenc_h, benc_h, wdec_h, bdec_h, fab, errb, attr,
           active, benc, bdec,
           X, G, wenc, wdec, wpeer, pre, acts, apeer, projt, part, r1, ra, rb, red, reu, rz, sums, got,
           local_sem, send, recv):
    tok, feat = lax.axis_index("tok"), lax.axis_index("feat")
    x, zh = tok // 2, tok % 2
    y, z, c = feat // 4, (feat // 2) % 2, feat % 2
    p = feat // 2
    up, dn, opp = (y + 1) % NY, (y + 3) % NY, (y + 2) % NY

    def at(yy, zz, cc):
        return {"tok": tok, "feat": yy * 4 + zz * 2 + cc}

    d_core, d_z, d_up, d_dn = at(y, z, 1 - c), at(y, 1 - z, c), at(up, z, c), at(dn, z, c)

    def tok_peer(dx, other):
        xx = (x + dx) % NX
        zz = 1 - zh if other else zh
        return xx * 2 + zz, (y * 2 + (1 - z if other else z)) * 2 + c

    peers = [(dx, o) for o in (0, 1) for dx in range(NX) if dx or o]
    barrier = pltpu.get_barrier_semaphore()
    for dx, o in peers:
        tt, ff = tok_peer(dx, o)
        pl.semaphore_signal(barrier, inc=1, device_id={"tok": tt, "feat": ff}, device_id_type=MESH)
    d_diag, d_opp = at(y, 1 - z, 1 - c), at(opp, z, c)
    group = (d_core, d_z, d_up, d_dn, d_diag, d_opp)
    for dev in group:
        pl.semaphore_signal(barrier, inc=1, device_id=dev, device_id_type=MESH)
    small = [pltpu.make_async_copy(s, d, local_sem.at[4 + i])
             for i, (s, d) in enumerate(((active_h, active), (benc_h, benc), (bdec_h, bdec)))]
    w1 = pltpu.make_async_copy(wenc_h, wenc, local_sem.at[0])
    w2 = pltpu.make_async_copy(wdec_h, wdec, local_sem.at[1])
    own = []
    for i, (src, dst) in enumerate(((xt, X), (gt, G))):
        own.append(pltpu.make_async_copy(
            src.at[:, pl.ds(pl.multiple_of(tok * ROWS, ROWS), ROWS)], dst.at[p, 0, x, c], local_sem.at[2 + i]))
        own[i].start()
    w1.start()
    for copy in small:
        copy.start()
    w2.start()

    with mark("barrier"):
        pl.semaphore_wait(barrier, len(peers) + len(group))

    cp = Copies(send, recv)
    for i, (src, dst) in enumerate(((xt, X), (gt, G))):
        for dx, o in ((1, 0), (3, 0), (0, 1), (1, 1), (3, 1), (2, 0), (2, 1)):
            tt, ff = tok_peer(dx, o)
            cp.start(f"t{o}{dx}" if i == 0 else f"tg{dx}" if o == 0 and dx != 2 else "tg",
                     src.at[:, pl.ds(pl.multiple_of(tt * ROWS, ROWS), ROWS)], dst.at[ff // 2, o, x, c],
                     {"tok": tt, "feat": ff}, 1)

    sent_wpeer = []

    def send_wpeer():
        q = len(sent_wpeer)
        sent_wpeer.append(q)
        cols = pl.ds(pl.multiple_of((q * 2 + 1 - c) * 512, 512), 512)
        cp.start(f"wpeer{q // 4}", wdec_h.at[:, cols], wpeer.at[q], d_core)

    def blk(buf, yy, zz, s, cc, part=None):
        if part is None:
            return buf.at[yy * 2 + zz, s, :, cc]
        return buf.at[yy * 2 + zz, s, part, cc]

    zo = 1 - z
    halves = (pl.ds(0, 2), pl.ds(2, 2))

    class Gather:
        def __init__(self, tag, buf, step):
            self.tag, self.buf, self.step, self.core = tag, buf, step, {}
            self.group = 0 if tag == "x" else 4

        def send(self, name, yy, zz, s, dev, part=None):
            b = blk(self.buf, yy, zz, s, c, part)
            cp.start(self.tag + name, b, b, dev, self.group)

        def wait(self, name, yy, zz, s, dev):
            cp.arrived(self.tag + name, blk(self.buf, yy, zz, s, c), dev)

        def to_core(self, name, yy, zz, s, part=None):
            b = blk(self.buf, yy, zz, s, c, part)
            cp.start(self.tag + name + "c", b, b, d_core, self.group)
            self.core[name] = (yy, zz, s)

        def steps(self, *names):
            for name in names:
                yy, zz, s = self.core[name]
                cp.arrived(self.tag + name + "c", blk(self.buf, yy, zz, s, 1 - c), d_core)
                with mark(f"s{self.tag}{name}"):
                    self.step(yy, zz, s)

        def begin(self):
            self.send("u1", y, z, 1, d_up)
            self.send("d1", y, z, 1, d_dn)
            self.begin_slab(0, (x + 2) % NX)
            self.send("z1", y, z, 1, d_z)
            self.to_core("o1", y, z, 1)

        def begin_slab(self, s, xx):
            self.send(f"u{s}", y, z, s, d_up, xx)
            self.send(f"d{s}", y, z, s, d_dn, xx)
            self.send(f"z{s}", y, z, s, d_z, xx)
            self.to_core(f"o{s}", y, z, s, xx)

        def a(self):
            self.wait("u1", dn, z, 1, d_dn)
            self.send("zu1", dn, z, 1, d_z)
            self.send("f1", dn, z, 1, d_up, halves[0])
            self.wait("d1", up, z, 1, d_up)
            self.send("zd1", up, z, 1, d_z)
            self.send("f1", up, z, 1, d_dn, halves[1])

        def b(self):
            self.wait("z0", y, zo, 0, d_z)
            self.send("uz", y, zo, 0, d_up)
            self.send("dz", y, zo, 0, d_dn)
            self.to_core("p0", y, zo, 0)

        def c(self):
            self.wait("u0", dn, z, 0, d_dn)
            self.send("f0", dn, z, 0, d_up, halves[0])
            self.wait("d0", up, z, 0, d_up)
            self.send("f0", up, z, 0, d_dn, halves[1])
            self.to_core("u0c", dn, z, 0)
            self.to_core("d0c", up, z, 0)
            self.to_core("u1c", dn, z, 1)
            self.to_core("d1c", up, z, 1)

        def c1(self):
            self.wait("z1", y, zo, 1, d_z)
            self.to_core("p1", y, zo, 1)

        def d(self):
            self.wait("f1", opp, z, 1, d_dn)
            self.send("zo1", opp, z, 1, d_z)
            self.to_core("op1", opp, z, 1)

        def e(self):
            self.wait("uz", dn, zo, 0, d_dn)
            self.send("fz", dn, zo, 0, d_up, halves[0])
            self.wait("dz", up, zo, 0, d_up)
            self.send("fz", up, zo, 0, d_dn, halves[1])
            self.to_core("uzc", dn, zo, 0)
            self.to_core("dzc", up, zo, 0)

        def f(self):
            self.wait("f0", opp, z, 0, d_dn)
            self.to_core("op0", opp, z, 0)

        def g(self):
            self.wait("zu1", dn, zo, 1, d_z)
            self.to_core("zu1c", dn, zo, 1)
            self.wait("zd1", up, zo, 1, d_z)
            self.to_core("zd1c", up, zo, 1)

        def h(self):
            self.wait("fz", opp, zo, 0, d_dn)
            self.to_core("opz", opp, zo, 0)

        def i(self):
            self.wait("zo1", opp, zo, 1, d_z)
            self.to_core("zo1c", opp, zo, 1)

    def place(yy, zz, s):
        if s == 0:
            return zh, yy * 2 + zz
        return 1 - zh, yy * 2 + 1 - zz

    pre[...] = jnp.zeros_like(pre)
    projt[...] = jnp.zeros_like(projt)

    def pre_step(yy, zz, s):
        zp, q = place(yy, zz, s)
        lhs = X[yy * 2 + zz, s].reshape(512, ROWS)
        rhs = wenc[:, zp, q].reshape(512, FD)
        pre[...] += lax.dot_general(lhs, rhs, (((0,), (0,)), ((), ())), preferred_element_type=F32)

    def proj_step(yy, zz, s):
        zp, q = place(yy, zz, s)
        lhs = jnp.concatenate(
            [wdec[:, pl.ds(pl.multiple_of((xx * 2 + zp) * 1024 + q * 128, 128), 128)] for xx in range(NX)], axis=1)
        projt[...] += jnp.dot(lhs, G[yy * 2 + zz, s].reshape(512, ROWS), preferred_element_type=F32)

    gx = Gather("x", X, pre_step)
    gg = Gather("g", G, proj_step)
    for o, dx in ((0, 0), (0, 1), (0, 3), (1, 0), (1, 1), (1, 3), (0, 2), (1, 2)):
        if dx or o:
            cp.arrived(f"t{o}{dx}", X.at[p, o, (x + NX - dx) % NX, c], d_z)
        else:
            own[0].wait()
        gx.begin_slab(o, (x + NX - dx) % NX)
        if dx == 0 and o == 0:
            own[1].wait()
            gg.begin_slab(0, x)
        if (o, dx) in ((0, 0), (0, 1), (1, 0)):
            send_wpeer()
    for dx in (1, 3):
        xx = (x + NX - dx) % NX
        cp.arrived(f"tg{dx}", G.at[p, 0, xx, c], d_z)
        gg.begin_slab(0, xx)
    send_wpeer()
    gx.a()
    gx.b()
    gx.c()
    send_wpeer()
    with mark("w1"):
        w1.wait()
        for copy in small:
            copy.wait()
    gx.steps("o0", "o1")
    gx.c1()
    send_wpeer()
    gx.steps("p0", "u0c")
    gx.d()
    send_wpeer()
    gx.steps("d0c")
    gx.e()
    cp.arrived("tg", G.at[pl.ds(0, 5), 0, 0, 0], d_z)
    gg.begin()
    send_wpeer()
    gx.steps("u1c", "d1c", "p1")
    gx.f()
    gx.g()
    gx.steps("op1", "uzc", "dzc", "op0")
    gx.h()
    gx.i()
    gg.a()
    gx.steps("zu1c", "zd1c")
    gg.b()
    gg.c()
    gx.steps("opz", "zo1c")

    with mark("acts"):
        lane_block = feat * 5 + lax.broadcasted_iota(jnp.int32, (1, FD), 1) // 128
        for tile in range(2):
            hit = jnp.zeros((1, FD), F32)
            for j in range(active.shape[1]):
                hit = jnp.where(lane_block == active[tile, j], 1.0, hit)
            rows = pl.ds(tile * 128, 128)
            acts[rows, :] = (jnp.maximum(pre[rows, :] + benc[...].reshape(1, FD), 0.0) * hit).astype(BF16)
    cp.start("acts", acts, apeer, d_core, 2)
    with mark("w2"):
        w2.wait()

    def share(q):
        cols = pl.ds(pl.multiple_of((q * 2 + c) * 512, 512), 512)
        lhs = jnp.concatenate([acts[...], apeer[...]], axis=1)
        rhs = jnp.concatenate([wdec[:, cols], wpeer[q]], axis=0)
        part[q] = jnp.dot(lhs, rhs, preferred_element_type=F32).astype(BF16)

    def add(dst, *srcs):
        total = dst[...].astype(F32)
        for s in srcs:
            total = total + s[...].astype(F32)
        dst[...] = total.astype(BF16)

    def unit(u, yy, lo, n):
        zz = (z, zo, z)[u]
        return part.at[yy * 2 + zz, pl.ds((0, N1, N1)[u] + lo, n)]

    rows_of, cut = (N1, N2, N2), (48, 80, 80)

    def land(buf, u, n):
        return buf.at[u, pl.ds(0, n)]

    def first(u):
        a, b = cut[u], rows_of[u] - cut[u]
        cp.start(f"a{u}", unit(u, opp, 0, a), land(ra, u, a), d_up, 4)
        cp.start(f"b{u}", unit(u, opp, a, b), land(rb, u, b), d_dn, 4)

    def second(u):
        n, a, b = rows_of[u], cut[u], rows_of[u] - cut[u]
        cp.arrived(f"a{u}", land(ra, u, a), d_dn)
        add(unit(u, up, 0, a), land(ra, u, a))
        cp.start(f"u{u}", unit(u, up, 0, n), land(red, u, n), d_up, 4)
        cp.arrived(f"b{u}", land(rb, u, b), d_up)
        add(unit(u, dn, a, b), land(rb, u, b))
        cp.start(f"d{u}", unit(u, dn, 0, n), land(reu, u, n), d_dn, 4)

    def third(u):
        cp.arrived(f"u{u}", land(red, u, rows_of[u]), d_dn)
        cp.arrived(f"d{u}", land(reu, u, rows_of[u]), d_up)

    rel = (opp, up, dn, y)

    def zsend(i):
        cp.start(f"z{i}", part.at[rel[i] * 2 + zo, pl.ds(0, N1)], r1.at[i], d_z, 4)

    def zadd(i):
        cp.arrived(f"z{i}", r1.at[i], d_z)
        add(part.at[rel[i] * 2 + z, pl.ds(0, N1)], r1.at[i])

    gg.steps("o0")
    gg.d()
    cp.arrived("acts", apeer, d_core)
    cp.arrived("wpeer0", wpeer.at[pl.ds(0, 4)], d_core)
    cp.arrived("wpeer1", wpeer.at[pl.ds(4, 4)], d_core)

    def shares(name, lo, n):
        with mark(name):
            @pl.loop(lo, lo + n)
            def _(i):
                k = i // 2
                yy = (y + k + k // 2) % NY if lo else opp
                share(yy * 2 + jnp.where(i % 2 == 0, zo, z))

    shares("share0", 0, 2)
    first(1)
    first(2)
    zsend(0)
    shares("share1", 2, 4)
    zsend(1)
    zsend(2)
    gg.e()
    gg.c1()
    gg.f()
    gg.g()
    shares("share2", 6, 2)
    zsend(3)
    gg.steps("o1", "p0")
    second(1)
    gg.i()
    gg.steps("u0c", "d0c", "u1c", "d1c", "p1")
    zadd(0)
    first(0)
    second(2)
    gg.steps("uzc", "dzc", "op1")
    gg.h()
    gg.steps("op0", "zu1c", "zd1c", "zo1c", "opz")
    with mark("err"):
        ox, oz = feat // 4, (feat // 2) % 2
        os = jnp.where(oz == zh, 0, 1)
        term = jnp.zeros((ROWS, 128), F32)
        bd = bdec[...].reshape(1, 512)
        for j in range(4):
            q = (feat % 2) * 4 + j
            pb = q + os * (1 - 2 * (q % 2))
            xs = X[pb, os, ox].reshape(128, ROWS).astype(F32).T - bd[:, j * 128:(j + 1) * 128]
            gs = G[pb, os, ox].reshape(128, ROWS).astype(F32).T
            errb[:, j * 128:(j + 1) * 128] = xs
            term = term + xs * gs
        for j in range(5):
            lanes = slice(j * 128, (j + 1) * 128)
            f = acts[:, lanes].astype(F32) * projt[lanes, :].T
            fab[:, lanes] = f
            term = term - f
        sums[0] = jnp.broadcast_to(jnp.sum(term.T, axis=0, keepdims=True), (8, ROWS))

    def exchange(key, src, slots, mine, devs):
        slots[mine] = src[...]
        for dev in devs:
            cp.start(key, src, slots.at[mine], dev, 3)

    def total(key, slots):
        cp.arrived(key, slots.at[pl.ds(0, 3)], d_z)
        return slots[0] + slots[1] + slots[2] + slots[3]

    exchange("s0", sums.at[0], got.at[0], z * 2 + c, (d_core, d_z, d_diag))
    third(1)
    add(unit(1, y, 0, N2), red.at[1], reu.at[1])
    cp.start("last", unit(1, y, 0, N2), rz, d_z, 4)
    zadd(1)
    zadd(2)
    second(0)
    sums[1] = total("s0", got.at[0])
    exchange("s1", sums.at[1], got.at[1], y, (d_up, d_dn, d_opp))
    zadd(3)
    third(2)
    hi = pl.ds(N1, N2)
    errb[hi, :] = errb[hi, :] - (unit(2, y, 0, N2)[...].astype(F32) + red[2].astype(F32) + reu[2].astype(F32))
    cp.arrived("last", rz, d_z)
    errb[hi, :] = errb[hi, :] - rz[...].astype(F32)
    third(0)
    lo = pl.ds(0, N1)
    errb[lo, :] = errb[lo, :] - (unit(0, y, 0, N1)[...].astype(F32) + red[0, lo].astype(F32) + reu[0, lo].astype(F32))
    attr[...] = total("s1", got.at[1])[0:1, :]
    with mark("drain"):
        assert len(cp.keys) == NRECV, len(cp.keys)
        cp.drain(0, lambda n: wdec.at[pl.ds(0, n)], 8192 * 2, d_z)
        cp.drain(4, lambda n: wdec.at[pl.ds(0, n)], 8192 * 2, d_z)
        cp.drain(1, lambda n: X.at[pl.ds(0, n), 0, 0], 65536, d_z)
        cp.drain(2, lambda n: acts, ROWS * FD * 2, d_z)
        cp.drain(3, lambda n: part.at[0, pl.ds(0, n)], 1024, d_z)


def write_out(fa, err, attr, fa_h, err_h, attr_h, sem):
    copies = [pltpu.make_async_copy(s, d, sem.at[i])
              for i, (s, d) in enumerate(((fa, fa_h), (err, err_h), (attr, attr_h)))]
    for copy in copies:
        copy.start()
    for copy in copies:
        copy.wait()


def per_device(resid, resid_grad, active, w_enc, b_enc, w_dec, b_dec):
    any_, vmem = pl.BlockSpec(memory_space=pl.ANY), pl.BlockSpec(memory_space=pltpu.VMEM)
    V = pltpu.VMEM
    outs = [((ROWS, FD), F32), ((ROWS, 512), F32), ((1, ROWS), F32)]
    held = pl.pallas_call(
        kernel,
        out_shape=tuple(V(*o) for o in outs),
        in_specs=[any_] * 7,
        out_specs=(vmem, vmem, vmem),
        scratch_shapes=[
            pltpu.SMEM(active.shape, active.dtype),
            V(b_enc.shape, F32),
            V(b_dec.shape, F32),
            V((8, 2, NX, 2, 64, ROWS), BF16),
            V((8, 2, NX, 2, 64, ROWS), BF16),
            V((NX, 2, 8, 128, FD), BF16),
            V((FD, 8192), BF16),
            V((8, FD, 512), BF16),
            V((ROWS, FD), F32),
            V((ROWS, FD), BF16),
            V((ROWS, FD), BF16),
            V((FD, ROWS), F32),
            V((8, ROWS, 512), BF16),
            V((NY, N1, 512), BF16),
            V((3, 80, 512), BF16),
            V((3, 80, 512), BF16),
            V((3, N2, 512), BF16),
            V((3, N2, 512), BF16),
            V((N2, 512), BF16),
            V((2, 8, ROWS), F32),
            V((2, 4, 8, ROWS), F32),
            pltpu.SemaphoreType.DMA((7,)),
            pltpu.SemaphoreType.DMA((5,)),
            pltpu.SemaphoreType.DMA((NRECV,)),
        ],
        compiler_params=pltpu.CompilerParams(
            collective_id=0, has_side_effects=True, vmem_limit_bytes=58 * 1024 * 1024),
    )(resid.T, resid_grad.T, active, w_enc.reshape(NX, 2, 8, 128, FD), b_enc, w_dec, b_dec)
    fa, err, attr = pl.pallas_call(
        write_out,
        out_shape=tuple(jax.ShapeDtypeStruct(*o) for o in outs),
        in_specs=[vmem] * 3,
        out_specs=(any_,) * 3,
        scratch_shapes=[pltpu.SemaphoreType.DMA((3,))],
    )(*(pltpu.with_memory_space_constraint(h, pltpu.VMEM) for h in held))
    return fa, err, attr.reshape(ROWS)


def solution(mesh):
    placed = (
        P(None, ("tok", "feat")),
        P(None, ("tok", "feat")),
        P("tok", None),
        P(None, "feat"),
        P("feat"),
        P("feat", None),
        P("feat"),
    )
    return jax.shard_map(
        per_device,
        mesh=mesh,
        in_specs=placed,
        out_specs=(P("tok", "feat"), P("tok", "feat"), P("tok")),
        check_vma=False,
    )
```

```python
import contextlib
import math

import jax
import jax.numpy as jnp
from jax import lax
from jax.experimental import pallas as pl
from jax.experimental.pallas import tpu as pltpu
from jax.sharding import PartitionSpec as P

MESH = pl.DeviceIdType.MESH
F32, BF16 = jnp.float32, jnp.bfloat16
NX, NY = 4, 4
ROWS = 256
FD = 640
NRECV = 92
N1, N2 = 96, 160
SCOPED = False


def mark(name):
    return jax.named_scope(name) if SCOPED else contextlib.nullcontext()


class Copies:
    def __init__(self, send, recv):
        self.send, self.recv, self.keys, self.sent = send, recv, {}, {}

    def start(self, key, src, dst, dev, group=0):
        k = self.keys.setdefault(key, len(self.keys))
        pltpu.make_async_remote_copy(
            src_ref=src, dst_ref=dst, send_sem=self.send.at[group], recv_sem=self.recv.at[k],
            device_id=dev, device_id_type=MESH,
        ).start()
        self.sent[group] = self.sent.get(group, 0) + math.prod(src.shape) * src.dtype.itemsize

    def arrived(self, key, mine, dev):
        with mark(f"w{key}"):
            pltpu.make_async_remote_copy(
                src_ref=mine, dst_ref=mine, send_sem=self.send.at[0], recv_sem=self.recv.at[self.keys[key]],
                device_id=dev, device_id_type=MESH,
            ).wait_recv()

    def drain(self, group, rows, row_bytes, dev):
        count, rest = divmod(self.sent[group], row_bytes)
        assert rest == 0
        mine = rows(count)
        pltpu.make_async_remote_copy(
            src_ref=mine, dst_ref=mine, send_sem=self.send.at[group], recv_sem=self.recv.at[0],
            device_id=dev, device_id_type=MESH,
        ).wait_send()


def kernel(xt, gt, active_h, wenc_h, benc_h, wdec_h, bdec_h, fab, errb, attr,
           active, benc, bdec,
           X, G, wenc, wdec, wpeer, pre, acts, apeer, projt, part, r1, ra, rb, red, reu, rz, sums, got,
           local_sem, send, recv):
    tok, feat = lax.axis_index("tok"), lax.axis_index("feat")
    x, zh = tok // 2, tok % 2
    y, z, c = feat // 4, (feat // 2) % 2, feat % 2
    p = feat // 2
    up, dn, opp = (y + 1) % NY, (y + 3) % NY, (y + 2) % NY

    def at(yy, zz, cc):
        return {"tok": tok, "feat": yy * 4 + zz * 2 + cc}

    d_core, d_z, d_up, d_dn = at(y, z, 1 - c), at(y, 1 - z, c), at(up, z, c), at(dn, z, c)

    def tok_peer(dx, other):
        xx = (x + dx) % NX
        zz = 1 - zh if other else zh
        return xx * 2 + zz, (y * 2 + (1 - z if other else z)) * 2 + c

    peers = [(dx, o) for o in (0, 1) for dx in range(NX) if dx or o]
    barrier = pltpu.get_barrier_semaphore()
    for dx, o in peers:
        tt, ff = tok_peer(dx, o)
        pl.semaphore_signal(barrier, inc=1, device_id={"tok": tt, "feat": ff}, device_id_type=MESH)
    d_diag, d_opp = at(y, 1 - z, 1 - c), at(opp, z, c)
    group = (d_core, d_z, d_up, d_dn, d_diag, d_opp)
    for dev in group:
        pl.semaphore_signal(barrier, inc=1, device_id=dev, device_id_type=MESH)
    small = [pltpu.make_async_copy(s, d, local_sem.at[4 + i])
             for i, (s, d) in enumerate(((active_h, active), (benc_h, benc), (bdec_h, bdec)))]
    w1 = pltpu.make_async_copy(wenc_h, wenc, local_sem.at[0])
    w2 = pltpu.make_async_copy(wdec_h, wdec, local_sem.at[1])
    own = []
    for i, (src, dst) in enumerate(((xt, X), (gt, G))):
        own.append(pltpu.make_async_copy(
            src.at[:, pl.ds(pl.multiple_of(tok * ROWS, ROWS), ROWS)], dst.at[p, 0, x, c], local_sem.at[2 + i]))
        own[i].start()
    w1.start()
    for copy in small:
        copy.start()
    w2.start()

    with mark("barrier"):
        pl.semaphore_wait(barrier, len(peers) + len(group))

    cp = Copies(send, recv)
    for i, (src, dst) in enumerate(((xt, X), (gt, G))):
        for dx, o in ((1, 0), (3, 0), (0, 1), (1, 1), (3, 1), (2, 0), (2, 1)):
            tt, ff = tok_peer(dx, o)
            cp.start(f"t{o}{dx}" if i == 0 else f"tg{dx}" if o == 0 and dx != 2 else "tg",
                     src.at[:, pl.ds(pl.multiple_of(tt * ROWS, ROWS), ROWS)], dst.at[ff // 2, o, x, c],
                     {"tok": tt, "feat": ff}, 1)

    sent_wpeer = []

    def send_wpeer():
        q = len(sent_wpeer)
        sent_wpeer.append(q)
        cols = pl.ds(pl.multiple_of((q * 2 + 1 - c) * 512, 512), 512)
        cp.start(f"wpeer{q // 4}", wdec_h.at[:, cols], wpeer.at[q], d_core)

    def blk(buf, yy, zz, s, cc, part=None):
        if part is None:
            return buf.at[yy * 2 + zz, s, :, cc]
        return buf.at[yy * 2 + zz, s, part, cc]

    zo = 1 - z
    halves = (pl.ds(0, 2), pl.ds(2, 2))

    class Gather:
        def __init__(self, tag, buf, step):
            self.tag, self.buf, self.step, self.core = tag, buf, step, {}
            self.group = 0 if tag == "x" else 4

        def send(self, name, yy, zz, s, dev, part=None):
            b = blk(self.buf, yy, zz, s, c, part)
            cp.start(self.tag + name, b, b, dev, self.group)

        def wait(self, name, yy, zz, s, dev):
            cp.arrived(self.tag + name, blk(self.buf, yy, zz, s, c), dev)

        def to_core(self, name, yy, zz, s, part=None):
            b = blk(self.buf, yy, zz, s, c, part)
            cp.start(self.tag + name + "c", b, b, d_core, self.group)
            self.core[name] = (yy, zz, s)

        def steps(self, *names):
            for name in names:
                yy, zz, s = self.core[name]
                cp.arrived(self.tag + name + "c", blk(self.buf, yy, zz, s, 1 - c), d_core)
                with mark(f"s{self.tag}{name}"):
                    self.step(yy, zz, s)

        def begin(self):
            self.send("u1", y, z, 1, d_up)
            self.send("d1", y, z, 1, d_dn)
            self.begin_slab(0, (x + 2) % NX)
            self.send("z1", y, z, 1, d_z)
            self.to_core("o1", y, z, 1)

        def begin_slab(self, s, xx):
            self.send(f"u{s}", y, z, s, d_up, xx)
            self.send(f"d{s}", y, z, s, d_dn, xx)
            self.send(f"z{s}", y, z, s, d_z, xx)
            self.to_core(f"o{s}", y, z, s, xx)

        def a(self):
            self.wait("u1", dn, z, 1, d_dn)
            self.send("zu1", dn, z, 1, d_z)
            self.send("f1", dn, z, 1, d_up, halves[0])
            self.wait("d1", up, z, 1, d_up)
            self.send("zd1", up, z, 1, d_z)
            self.send("f1", up, z, 1, d_dn, halves[1])

        def b(self):
            self.wait("z0", y, zo, 0, d_z)
            self.send("uz", y, zo, 0, d_up)
            self.send("dz", y, zo, 0, d_dn)
            self.to_core("p0", y, zo, 0)

        def c(self):
            self.wait("u0", dn, z, 0, d_dn)
            self.send("f0", dn, z, 0, d_up, halves[0])
            self.wait("d0", up, z, 0, d_up)
            self.send("f0", up, z, 0, d_dn, halves[1])
            self.to_core("u0c", dn, z, 0)
            self.to_core("d0c", up, z, 0)
            self.to_core("u1c", dn, z, 1)
            self.to_core("d1c", up, z, 1)

        def c1(self):
            self.wait("z1", y, zo, 1, d_z)
            self.to_core("p1", y, zo, 1)

        def d(self):
            self.wait("f1", opp, z, 1, d_dn)
            self.send("zo1", opp, z, 1, d_z)
            self.to_core("op1", opp, z, 1)

        def e(self):
            self.wait("uz", dn, zo, 0, d_dn)
            self.send("fz", dn, zo, 0, d_up, halves[0])
            self.wait("dz", up, zo, 0, d_up)
            self.send("fz", up, zo, 0, d_dn, halves[1])
            self.to_core("uzc", dn, zo, 0)
            self.to_core("dzc", up, zo, 0)

        def f(self):
            self.wait("f0", opp, z, 0, d_dn)
            self.to_core("op0", opp, z, 0)

        def g(self):
            self.wait("zu1", dn, zo, 1, d_z)
            self.to_core("zu1c", dn, zo, 1)
            self.wait("zd1", up, zo, 1, d_z)
            self.to_core("zd1c", up, zo, 1)

        def h(self):
            self.wait("fz", opp, zo, 0, d_dn)
            self.to_core("opz", opp, zo, 0)

        def i(self):
            self.wait("zo1", opp, zo, 1, d_z)
            self.to_core("zo1c", opp, zo, 1)

    def place(yy, zz, s):
        if s == 0:
            return zh, yy * 2 + zz
        return 1 - zh, yy * 2 + 1 - zz

    pre[...] = jnp.zeros_like(pre)
    projt[...] = jnp.zeros_like(projt)

    def pre_step(yy, zz, s):
        zp, q = place(yy, zz, s)
        lhs = X[yy * 2 + zz, s].reshape(512, ROWS)
        rhs = wenc[:, zp, q].reshape(512, FD)
        pre[...] += lax.dot_general(lhs, rhs, (((0,), (0,)), ((), ())), preferred_element_type=F32)

    def proj_step(yy, zz, s):
        zp, q = place(yy, zz, s)
        lhs = jnp.concatenate(
            [wdec[:, pl.ds(pl.multiple_of((xx * 2 + zp) * 1024 + q * 128, 128), 128)] for xx in range(NX)], axis=1)
        projt[...] += jnp.dot(lhs, G[yy * 2 + zz, s].reshape(512, ROWS), preferred_element_type=F32)

    gx = Gather("x", X, pre_step)
    gg = Gather("g", G, proj_step)
    for o, dx in ((0, 0), (0, 1), (0, 3), (1, 0), (1, 1), (1, 3), (0, 2), (1, 2)):
        if dx or o:
            cp.arrived(f"t{o}{dx}", X.at[p, o, (x + NX - dx) % NX, c], d_z)
        else:
            own[0].wait()
        gx.begin_slab(o, (x + NX - dx) % NX)
        if dx == 0 and o == 0:
            own[1].wait()
            gg.begin_slab(0, x)
        if (o, dx) in ((0, 0), (0, 1), (1, 0), (1, 1)):
            send_wpeer()
    for dx in (1, 3):
        xx = (x + NX - dx) % NX
        cp.arrived(f"tg{dx}", G.at[p, 0, xx, c], d_z)
        gg.begin_slab(0, xx)
    send_wpeer()
    send_wpeer()
    gx.a()
    gx.b()
    gx.c()
    with mark("w1"):
        w1.wait()
        for copy in small:
            copy.wait()
    gx.steps("o0", "o1")
    gx.c1()
    gx.steps("p0", "u0c")
    gx.d()
    gx.steps("d0c")
    gx.e()
    cp.arrived("tg", G.at[pl.ds(0, 5), 0, 0, 0], d_z)
    gg.begin()
    send_wpeer()
    gx.steps("u1c", "d1c", "p1")
    gx.f()
    gx.g()
    send_wpeer()
    gx.steps("op1", "uzc", "dzc", "op0")
    gx.h()
    gx.i()
    gg.b()
    gg.a()
    gx.steps("zu1c", "zd1c")
    gg.c()
    gx.steps("opz", "zo1c")

    with mark("acts"):
        lane_block = feat * 5 + lax.broadcasted_iota(jnp.int32, (1, FD), 1) // 128
        for tile in range(2):
            hit = jnp.zeros((1, FD), F32)
            for j in range(active.shape[1]):
                hit = jnp.where(lane_block == active[tile, j], 1.0, hit)
            rows = pl.ds(tile * 128, 128)
            acts[rows, :] = (jnp.maximum(pre[rows, :] + benc[...].reshape(1, FD), 0.0) * hit).astype(BF16)
    cp.start("acts", acts, apeer, d_core, 2)
    with mark("w2"):
        w2.wait()

    def share(q):
        cols = pl.ds(pl.multiple_of((q * 2 + c) * 512, 512), 512)
        lhs = jnp.concatenate([acts[...], apeer[...]], axis=1)
        rhs = jnp.concatenate([wdec[:, cols], wpeer[q]], axis=0)
        part[q] = jnp.dot(lhs, rhs, preferred_element_type=F32).astype(BF16)

    def add(dst, *srcs):
        total = dst[...].astype(F32)
        for s in srcs:
            total = total + s[...].astype(F32)
        dst[...] = total.astype(BF16)

    def unit(u, yy, lo, n):
        zz = (z, zo, z)[u]
        return part.at[yy * 2 + zz, pl.ds((0, N1, N1)[u] + lo, n)]

    rows_of, cut = (N1, N2, N2), (48, 80, 80)

    def land(buf, u, n):
        return buf.at[u, pl.ds(0, n)]

    def first(u):
        a, b = cut[u], rows_of[u] - cut[u]
        cp.start(f"a{u}", unit(u, opp, 0, a), land(ra, u, a), d_up, 4)
        cp.start(f"b{u}", unit(u, opp, a, b), land(rb, u, b), d_dn, 4)

    def second(u):
        n, a, b = rows_of[u], cut[u], rows_of[u] - cut[u]
        cp.arrived(f"a{u}", land(ra, u, a), d_dn)
        add(unit(u, up, 0, a), land(ra, u, a))
        cp.start(f"u{u}", unit(u, up, 0, n), land(red, u, n), d_up, 4)
        cp.arrived(f"b{u}", land(rb, u, b), d_up)
        add(unit(u, dn, a, b), land(rb, u, b))
        cp.start(f"d{u}", unit(u, dn, 0, n), land(reu, u, n), d_dn, 4)

    def third(u):
        cp.arrived(f"u{u}", land(red, u, rows_of[u]), d_dn)
        cp.arrived(f"d{u}", land(reu, u, rows_of[u]), d_up)

    rel = (opp, up, dn, y)

    def zsend(i):
        cp.start(f"z{i}", part.at[rel[i] * 2 + zo, pl.ds(0, N1)], r1.at[i], d_z, 4)

    def zadd(i):
        cp.arrived(f"z{i}", r1.at[i], d_z)
        add(part.at[rel[i] * 2 + z, pl.ds(0, N1)], r1.at[i])

    gg.steps("o0")
    cp.arrived("acts", apeer, d_core)
    cp.arrived("wpeer0", wpeer.at[pl.ds(0, 4)], d_core)
    cp.arrived("wpeer1", wpeer.at[pl.ds(4, 4)], d_core)

    def shares(name, lo, n):
        with mark(name):
            @pl.loop(lo, lo + n)
            def _(i):
                k = i // 2
                yy = (y + k + k // 2) % NY if lo else opp
                share(yy * 2 + jnp.where(i % 2 == 0, zo, z))

    shares("share0", 0, 2)
    first(1)
    first(2)
    gg.d()
    zsend(0)
    shares("share1", 2, 4)
    zsend(1)
    zsend(2)
    gg.e()
    gg.c1()
    gg.f()
    gg.g()
    shares("share2", 6, 2)
    zsend(3)
    gg.steps("o1", "p0")
    second(1)
    gg.i()
    gg.steps("u0c", "d0c", "u1c", "d1c", "p1")
    zadd(0)
    first(0)
    second(2)
    gg.steps("uzc", "dzc", "op1")
    gg.h()
    gg.steps("op0", "zu1c", "zd1c", "zo1c", "opz")
    with mark("err"):
        ox, oz = feat // 4, (feat // 2) % 2
        os = jnp.where(oz == zh, 0, 1)
        term = jnp.zeros((ROWS, 128), F32)
        bd = bdec[...].reshape(1, 512)
        for j in range(4):
            q = (feat % 2) * 4 + j
            pb = q + os * (1 - 2 * (q % 2))
            xs = X[pb, os, ox].reshape(128, ROWS).astype(F32).T - bd[:, j * 128:(j + 1) * 128]
            gs = G[pb, os, ox].reshape(128, ROWS).astype(F32).T
            errb[:, j * 128:(j + 1) * 128] = xs
            term = term + xs * gs
        for j in range(5):
            lanes = slice(j * 128, (j + 1) * 128)
            f = acts[:, lanes].astype(F32) * projt[lanes, :].T
            fab[:, lanes] = f
            term = term - f
        sums[0] = jnp.broadcast_to(jnp.sum(term.T, axis=0, keepdims=True), (8, ROWS))

    def exchange(key, src, slots, mine, devs):
        slots[mine] = src[...]
        for dev in devs:
            cp.start(key, src, slots.at[mine], dev, 3)

    def total(key, slots):
        cp.arrived(key, slots.at[pl.ds(0, 3)], d_z)
        return slots[0] + slots[1] + slots[2] + slots[3]

    exchange("s0", sums.at[0], got.at[0], z * 2 + c, (d_core, d_z, d_diag))
    third(1)
    add(unit(1, y, 0, N2), red.at[1], reu.at[1])
    cp.start("last", unit(1, y, 0, N2), rz, d_z, 4)
    zadd(1)
    zadd(2)
    second(0)
    sums[1] = total("s0", got.at[0])
    exchange("s1", sums.at[1], got.at[1], y, (d_up, d_dn, d_opp))
    zadd(3)
    third(2)
    hi = pl.ds(N1, N2)
    errb[hi, :] = errb[hi, :] - (unit(2, y, 0, N2)[...].astype(F32) + red[2].astype(F32) + reu[2].astype(F32))
    cp.arrived("last", rz, d_z)
    errb[hi, :] = errb[hi, :] - rz[...].astype(F32)
    third(0)
    lo = pl.ds(0, N1)
    errb[lo, :] = errb[lo, :] - (unit(0, y, 0, N1)[...].astype(F32) + red[0, lo].astype(F32) + reu[0, lo].astype(F32))
    attr[...] = total("s1", got.at[1])[0:1, :]
    with mark("drain"):
        assert len(cp.keys) == NRECV, len(cp.keys)
        cp.drain(0, lambda n: wdec.at[pl.ds(0, n)], 8192 * 2, d_z)
        cp.drain(4, lambda n: wdec.at[pl.ds(0, n)], 8192 * 2, d_z)
        cp.drain(1, lambda n: X.at[pl.ds(0, n), 0, 0], 65536, d_z)
        cp.drain(2, lambda n: acts, ROWS * FD * 2, d_z)
        cp.drain(3, lambda n: part.at[0, pl.ds(0, n)], 1024, d_z)


def write_out(fa, err, attr, fa_h, err_h, attr_h, sem):
    cuts = [pl.ds(i * 64, 64) for i in range(ROWS // 64)]
    pairs = [(s.at[r], d.at[r]) for s, d in ((fa, fa_h), (err, err_h)) for r in cuts] + [(attr, attr_h)]
    copies = [pltpu.make_async_copy(s, d, sem.at[i]) for i, (s, d) in enumerate(pairs)]
    for copy in copies:
        copy.start()
    for copy in copies:
        copy.wait()


def per_device(resid, resid_grad, active, w_enc, b_enc, w_dec, b_dec):
    any_, vmem = pl.BlockSpec(memory_space=pl.ANY), pl.BlockSpec(memory_space=pltpu.VMEM)
    V = pltpu.VMEM
    outs = [((ROWS, FD), F32), ((ROWS, 512), F32), ((1, ROWS), F32)]
    held = pl.pallas_call(
        kernel,
        out_shape=tuple(V(*o) for o in outs),
        in_specs=[any_] * 7,
        out_specs=(vmem, vmem, vmem),
        scratch_shapes=[
            pltpu.SMEM(active.shape, active.dtype),
            V(b_enc.shape, F32),
            V(b_dec.shape, F32),
            V((8, 2, NX, 2, 64, ROWS), BF16),
            V((8, 2, NX, 2, 64, ROWS), BF16),
            V((NX, 2, 8, 128, FD), BF16),
            V((FD, 8192), BF16),
            V((8, FD, 512), BF16),
            V((ROWS, FD), F32),
            V((ROWS, FD), BF16),
            V((ROWS, FD), BF16),
            V((FD, ROWS), F32),
            V((8, ROWS, 512), BF16),
            V((NY, N1, 512), BF16),
            V((3, 80, 512), BF16),
            V((3, 80, 512), BF16),
            V((3, N2, 512), BF16),
            V((3, N2, 512), BF16),
            V((N2, 512), BF16),
            V((2, 8, ROWS), F32),
            V((2, 4, 8, ROWS), F32),
            pltpu.SemaphoreType.DMA((7,)),
            pltpu.SemaphoreType.DMA((5,)),
            pltpu.SemaphoreType.DMA((NRECV,)),
        ],
        compiler_params=pltpu.CompilerParams(
            collective_id=0, has_side_effects=True, vmem_limit_bytes=58 * 1024 * 1024),
    )(resid.T, resid_grad.T, active, w_enc.reshape(NX, 2, 8, 128, FD), b_enc, w_dec, b_dec)
    fa, err, attr = pl.pallas_call(
        write_out,
        out_shape=tuple(jax.ShapeDtypeStruct(*o) for o in outs),
        in_specs=[vmem] * 3,
        out_specs=(any_,) * 3,
        scratch_shapes=[pltpu.SemaphoreType.DMA((9,))],
    )(*(pltpu.with_memory_space_constraint(h, pltpu.VMEM) for h in held))
    return fa, err, attr.reshape(ROWS)


def solution(mesh):
    placed = (
        P(None, ("tok", "feat")),
        P(None, ("tok", "feat")),
        P("tok", None),
        P(None, "feat"),
        P("feat"),
        P("feat", None),
        P("feat"),
    )
    return jax.shard_map(
        per_device,
        mesh=mesh,
        in_specs=placed,
        out_specs=(P("tok", "feat"), P("tok", "feat"), P("tok")),
        check_vma=False,
    )
```

```python
import contextlib
import math

import jax
import jax.numpy as jnp
from jax import lax
from jax.experimental import pallas as pl
from jax.experimental.pallas import tpu as pltpu
from jax.sharding import PartitionSpec as P

MESH = pl.DeviceIdType.MESH
F32, BF16 = jnp.float32, jnp.bfloat16
NX, NY = 4, 4
ROWS = 256
FD = 640
NRECV = 88
N1, N2 = 96, 160
SCOPED = False


def mark(name):
    return jax.named_scope(name) if SCOPED else contextlib.nullcontext()


class Copies:
    def __init__(self, send, recv):
        self.send, self.recv, self.keys, self.sent = send, recv, {}, {}

    def start(self, key, src, dst, dev, group=0):
        k = self.keys.setdefault(key, len(self.keys))
        pltpu.make_async_remote_copy(
            src_ref=src, dst_ref=dst, send_sem=self.send.at[group], recv_sem=self.recv.at[k],
            device_id=dev, device_id_type=MESH,
        ).start()
        self.sent[group] = self.sent.get(group, 0) + math.prod(src.shape) * src.dtype.itemsize

    def arrived(self, key, mine, dev):
        with mark(f"w{key}"):
            pltpu.make_async_remote_copy(
                src_ref=mine, dst_ref=mine, send_sem=self.send.at[0], recv_sem=self.recv.at[self.keys[key]],
                device_id=dev, device_id_type=MESH,
            ).wait_recv()

    def drain(self, group, rows, row_bytes, dev):
        count, rest = divmod(self.sent[group], row_bytes)
        assert rest == 0
        mine = rows(count)
        pltpu.make_async_remote_copy(
            src_ref=mine, dst_ref=mine, send_sem=self.send.at[group], recv_sem=self.recv.at[0],
            device_id=dev, device_id_type=MESH,
        ).wait_send()


def kernel(xt, gt, active_h, wenc_h, benc_h, wdec_h, bdec_h, fab, errb, attr,
           active, benc, bdec,
           X, G, wenc, wdec, wpeer, pre, acts, apeer, projt, part, r1, ra, rb, red, reu, rz, sums, got,
           local_sem, send, recv):
    tok, feat = lax.axis_index("tok"), lax.axis_index("feat")
    x, zh = tok // 2, tok % 2
    y, z, c = feat // 4, (feat // 2) % 2, feat % 2
    p = feat // 2
    up, dn, opp = (y + 1) % NY, (y + 3) % NY, (y + 2) % NY

    def at(yy, zz, cc):
        return {"tok": tok, "feat": yy * 4 + zz * 2 + cc}

    d_core, d_z, d_up, d_dn = at(y, z, 1 - c), at(y, 1 - z, c), at(up, z, c), at(dn, z, c)

    def tok_peer(dx, other):
        xx = (x + dx) % NX
        zz = 1 - zh if other else zh
        return xx * 2 + zz, (y * 2 + (1 - z if other else z)) * 2 + c

    peers = [(dx, o) for o in (0, 1) for dx in range(NX) if dx or o]
    barrier = pltpu.get_barrier_semaphore()
    for dx, o in peers:
        tt, ff = tok_peer(dx, o)
        pl.semaphore_signal(barrier, inc=1, device_id={"tok": tt, "feat": ff}, device_id_type=MESH)
    d_diag, d_opp = at(y, 1 - z, 1 - c), at(opp, z, c)
    group = (d_core, d_z, d_up, d_dn, d_diag, d_opp)
    for dev in group:
        pl.semaphore_signal(barrier, inc=1, device_id=dev, device_id_type=MESH)
    small = [pltpu.make_async_copy(s, d, local_sem.at[4 + i])
             for i, (s, d) in enumerate(((active_h, active), (benc_h, benc), (bdec_h, bdec)))]
    w1 = pltpu.make_async_copy(wenc_h, wenc, local_sem.at[0])
    w2 = pltpu.make_async_copy(wdec_h, wdec, local_sem.at[1])
    own = []
    for i, (src, dst) in enumerate(((xt, X), (gt, G))):
        own.append(pltpu.make_async_copy(
            src.at[:, pl.ds(pl.multiple_of(tok * ROWS, ROWS), ROWS)], dst.at[p, 0, x, c], local_sem.at[2 + i]))
        own[i].start()
    w1.start()
    for copy in small:
        copy.start()
    w2.start()

    with mark("barrier"):
        pl.semaphore_wait(barrier, len(peers) + len(group))

    cp = Copies(send, recv)
    for i, (src, dst) in enumerate(((xt, X), (gt, G))):
        for dx, o in ((1, 0), (3, 0), (0, 1), (1, 1), (3, 1), (2, 0), (2, 1)):
            tt, ff = tok_peer(dx, o)
            cp.start(f"t{o}{dx}" if i == 0 else f"tg{dx}" if o == 0 and dx != 2 else "tg",
                     src.at[:, pl.ds(pl.multiple_of(tt * ROWS, ROWS), ROWS)], dst.at[ff // 2, o, x, c],
                     {"tok": tt, "feat": ff}, 1)

    sent_wpeer = []

    def send_wpeer():
        q = len(sent_wpeer)
        sent_wpeer.append(q)
        cols = pl.ds(pl.multiple_of((q * 2 + 1 - c) * 512, 512), 512)
        cp.start("wpeer", wdec_h.at[:, cols], wpeer.at[q], d_core)

    def blk(buf, yy, zz, s, cc, part=None):
        if part is None:
            return buf.at[yy * 2 + zz, s, :, cc]
        return buf.at[yy * 2 + zz, s, part, cc]

    zo = 1 - z
    halves = (pl.ds(0, 2), pl.ds(2, 2))

    class Gather:
        def __init__(self, tag, buf, step):
            self.tag, self.buf, self.step, self.core = tag, buf, step, {}
            self.group = 0 if tag == "x" else 4

        def send(self, name, yy, zz, s, dev, part=None):
            b = blk(self.buf, yy, zz, s, c, part)
            cp.start(self.tag + name, b, b, dev, self.group)

        def wait(self, name, yy, zz, s, dev):
            cp.arrived(self.tag + name, blk(self.buf, yy, zz, s, c), dev)

        def to_core(self, name, yy, zz, s, part=None):
            b = blk(self.buf, yy, zz, s, c, part)
            cp.start(self.tag + name + "c", b, b, d_core, self.group)
            self.core[name] = (yy, zz, s)

        def steps(self, *names):
            for name in names:
                yy, zz, s = self.core[name]
                cp.arrived(self.tag + name + "c", blk(self.buf, yy, zz, s, 1 - c), d_core)
                with mark(f"s{self.tag}{name}"):
                    self.step(yy, zz, s)

        def begin(self):
            self.send("u1", y, z, 1, d_up)
            self.send("d1", y, z, 1, d_dn)
            self.begin_slab(0, (x + 2) % NX)
            self.send("z1", y, z, 1, d_z)
            self.to_core("o1", y, z, 1)

        def begin_slab(self, s, xx):
            self.send(f"u{s}", y, z, s, d_up, xx)
            self.send(f"d{s}", y, z, s, d_dn, xx)
            self.send(f"z{s}", y, z, s, d_z, xx)
            self.to_core(f"o{s}", y, z, s, xx)

        def a(self):
            self.wait("u1", dn, z, 1, d_dn)
            self.send("zu1", dn, z, 1, d_z)
            self.send("f1", dn, z, 1, d_up, halves[0])
            self.wait("d1", up, z, 1, d_up)
            self.send("zd1", up, z, 1, d_z)
            self.send("f1", up, z, 1, d_dn, halves[1])

        def b(self):
            self.wait("z0", y, zo, 0, d_z)
            self.send("uz", y, zo, 0, d_up)
            self.send("dz", y, zo, 0, d_dn)
            self.to_core("p0", y, zo, 0)

        def c(self):
            self.wait("u0", dn, z, 0, d_dn)
            self.send("f0", dn, z, 0, d_up, halves[0])
            self.wait("d0", up, z, 0, d_up)
            self.send("f0", up, z, 0, d_dn, halves[1])
            self.to_core("u0c", dn, z, 0)
            self.to_core("d0c", up, z, 0)
            self.to_core("u1c", dn, z, 1)
            self.to_core("d1c", up, z, 1)

        def c1(self):
            self.wait("z1", y, zo, 1, d_z)
            self.to_core("p1", y, zo, 1)

        def d(self):
            self.wait("f1", opp, z, 1, d_dn)
            self.send("zo1", opp, z, 1, d_z)
            self.to_core("op1", opp, z, 1)

        def e(self):
            self.wait("uz", dn, zo, 0, d_dn)
            self.send("fz", dn, zo, 0, d_up, halves[0])
            self.wait("dz", up, zo, 0, d_up)
            self.send("fz", up, zo, 0, d_dn, halves[1])
            self.to_core("uzc", dn, zo, 0)
            self.to_core("dzc", up, zo, 0)

        def f(self):
            self.wait("f0", opp, z, 0, d_dn)
            self.to_core("op0", opp, z, 0)

        def g(self):
            self.wait("zu1", dn, zo, 1, d_z)
            self.to_core("zu1c", dn, zo, 1)
            self.wait("zd1", up, zo, 1, d_z)
            self.to_core("zd1c", up, zo, 1)

        def h(self):
            self.wait("fz", opp, zo, 0, d_dn)
            self.to_core("opz", opp, zo, 0)

        def i(self):
            self.wait("zo1", opp, zo, 1, d_z)
            self.to_core("zo1c", opp, zo, 1)

    def place(yy, zz, s):
        if s == 0:
            return zh, yy * 2 + zz
        return 1 - zh, yy * 2 + 1 - zz

    pre[...] = jnp.zeros_like(pre)
    projt[...] = jnp.zeros_like(projt)

    def pre_step(yy, zz, s):
        zp, q = place(yy, zz, s)
        lhs = X[yy * 2 + zz, s].reshape(512, ROWS)
        rhs = wenc[:, zp, q].reshape(512, FD)
        pre[...] += lax.dot_general(lhs, rhs, (((0,), (0,)), ((), ())), preferred_element_type=F32)

    def proj_step(yy, zz, s):
        zp, q = place(yy, zz, s)
        lhs = jnp.concatenate(
            [wdec[:, pl.ds(pl.multiple_of((xx * 2 + zp) * 1024 + q * 128, 128), 128)] for xx in range(NX)], axis=1)
        projt[...] += jnp.dot(lhs, G[yy * 2 + zz, s].reshape(512, ROWS), preferred_element_type=F32)

    gx = Gather("x", X, pre_step)
    gg = Gather("g", G, proj_step)
    for o, dx in ((0, 0), (0, 1), (0, 3), (1, 0), (1, 1), (1, 3), (0, 2), (1, 2)):
        if dx or o:
            cp.arrived(f"t{o}{dx}", X.at[p, o, (x + NX - dx) % NX, c], d_z)
        else:
            own[0].wait()
        gx.begin_slab(o, (x + NX - dx) % NX)
        if dx == 0 and o == 0:
            own[1].wait()
            gg.begin_slab(0, x)
        if (o, dx) in ((0, 0), (0, 1), (1, 0)):
            send_wpeer()
    for dx in (1, 3):
        xx = (x + NX - dx) % NX
        cp.arrived(f"tg{dx}", G.at[p, 0, xx, c], d_z)
        gg.begin_slab(0, xx)
    send_wpeer()
    gx.a()
    gx.b()
    gx.c()
    send_wpeer()
    with mark("w1"):
        w1.wait()
        for copy in small:
            copy.wait()
    gx.steps("o0", "o1")
    gx.c1()
    send_wpeer()
    gx.steps("p0", "u0c")
    gx.d()
    send_wpeer()
    gx.steps("d0c")
    gx.e()
    cp.arrived("tg", G.at[pl.ds(0, 5), 0, 0, 0], d_z)
    gg.begin()
    send_wpeer()
    gx.steps("u1c", "d1c", "p1")
    gx.f()
    gx.g()
    gx.steps("op1", "uzc", "dzc", "op0")
    gx.h()
    gx.i()
    gg.a()
    gx.steps("zu1c", "zd1c")
    gg.b()
    gg.c()
    gx.steps("opz", "zo1c")

    with mark("acts"):
        lane_block = feat * 5 + lax.broadcasted_iota(jnp.int32, (1, FD), 1) // 128
        for tile in range(2):
            hit = jnp.zeros((1, FD), F32)
            for j in range(active.shape[1]):
                hit = jnp.where(lane_block == active[tile, j], 1.0, hit)
            rows = pl.ds(tile * 128, 128)
            acts[rows, :] = (jnp.maximum(pre[rows, :] + benc[...].reshape(1, FD), 0.0) * hit).astype(BF16)
    cp.start("acts", acts, apeer, d_core, 2)
    with mark("w2"):
        w2.wait()

    def share(q):
        cols = pl.ds(pl.multiple_of((q * 2 + c) * 512, 512), 512)
        lhs = jnp.concatenate([acts[...], apeer[...]], axis=1)
        rhs = jnp.concatenate([wdec[:, cols], wpeer[q]], axis=0)
        part[q] = jnp.dot(lhs, rhs, preferred_element_type=F32).astype(BF16)

    def add(dst, *srcs):
        total = dst[...].astype(F32)
        for s in srcs:
            total = total + s[...].astype(F32)
        dst[...] = total.astype(BF16)

    def unit(u, yy, lo, n):
        zz = (z, zo, z)[u]
        return part.at[yy * 2 + zz, pl.ds((0, N1, N1)[u] + lo, n)]

    rows_of, cut = (N1, N2, N2), (48, 80, 80)

    def land(buf, u, n):
        return buf.at[u, pl.ds(0, n)]

    def first(u):
        a, b = cut[u], rows_of[u] - cut[u]
        cp.start(f"a{u}", unit(u, opp, 0, a), land(ra, u, a), d_up, 4)
        cp.start(f"b{u}", unit(u, opp, a, b), land(rb, u, b), d_dn, 4)

    def second(u):
        n, a, b = rows_of[u], cut[u], rows_of[u] - cut[u]
        cp.arrived(f"a{u}", land(ra, u, a), d_dn)
        add(unit(u, up, 0, a), land(ra, u, a))
        cp.start(f"e{u}", unit(u, up, 0, n), land(red, u, n), d_up, 4)
        cp.arrived(f"b{u}", land(rb, u, b), d_up)
        add(unit(u, dn, a, b), land(rb, u, b))
        cp.start(f"e{u}", unit(u, dn, 0, n), land(reu, u, n), d_dn, 4)

    def third(u):
        cp.arrived(f"e{u}", part.at[pl.ds(0, 2), pl.ds(0, rows_of[u])], d_dn)

    rel = (opp, up, dn, y)

    def zsend(i):
        cp.start(f"z{i}", part.at[rel[i] * 2 + zo, pl.ds(0, N1)], r1.at[i], d_z, 4)

    def zadd(i):
        cp.arrived(f"z{i}", r1.at[i], d_z)
        add(part.at[rel[i] * 2 + z, pl.ds(0, N1)], r1.at[i])

    gg.steps("o0")
    gg.d()
    ox, oz = feat // 4, (feat // 2) % 2
    os = jnp.where(oz == zh, 0, 1)
    bd = bdec[...].reshape(1, 512)
    for j in range(4):
        q = (feat % 2) * 4 + j
        pb = q + os * (1 - 2 * (q % 2))
        xs = X[pb, os, ox].reshape(128, ROWS).astype(F32).T
        errb[:, j * 128:(j + 1) * 128] = xs - bd[:, j * 128:(j + 1) * 128]
    cp.arrived("acts", apeer, d_core)
    cp.arrived("wpeer", wpeer, d_core)

    def shares(name, lo, n):
        with mark(name):
            @pl.loop(lo, lo + n)
            def _(i):
                k = i // 2
                yy = (y + k + k // 2) % NY if lo else opp
                share(yy * 2 + jnp.where(i % 2 == 0, zo, z))

    shares("share0", 0, 2)
    first(1)
    first(2)
    zsend(0)
    shares("share1", 2, 4)
    zsend(1)
    zsend(2)
    gg.e()
    gg.c1()
    gg.f()
    gg.g()
    shares("share2", 6, 2)
    zsend(3)
    gg.steps("o1", "p0")
    second(1)
    gg.i()
    gg.steps("u0c", "d0c", "u1c", "d1c", "p1")
    zadd(0)
    first(0)
    second(2)
    gg.steps("uzc", "dzc", "op1")
    gg.h()
    gg.steps("op0", "zu1c", "zd1c", "zo1c", "opz")
    with mark("err"):
        term = jnp.zeros((ROWS, 128), F32)
        for j in range(4):
            q = (feat % 2) * 4 + j
            pb = q + os * (1 - 2 * (q % 2))
            gs = G[pb, os, ox].reshape(128, ROWS).astype(F32).T
            term = term + errb[:, j * 128:(j + 1) * 128] * gs
        for j in range(5):
            lanes = slice(j * 128, (j + 1) * 128)
            f = acts[:, lanes].astype(F32) * projt[lanes, :].T
            fab[:, lanes] = f
            term = term - f
        sums[0] = jnp.broadcast_to(jnp.sum(term.T, axis=0, keepdims=True), (8, ROWS))

    def exchange(key, src, slots, mine, devs):
        slots[mine] = src[...]
        for dev in devs:
            cp.start(key, src, slots.at[mine], dev, 3)

    def total(key, slots):
        cp.arrived(key, slots.at[pl.ds(0, 3)], d_z)
        return slots[0] + slots[1] + slots[2] + slots[3]

    exchange("s0", sums.at[0], got.at[0], z * 2 + c, (d_core, d_z, d_diag))
    third(1)
    add(unit(1, y, 0, N2), red.at[1], reu.at[1])
    cp.start("last", unit(1, y, 0, N2), rz, d_z, 4)
    zadd(1)
    zadd(2)
    second(0)
    sums[1] = total("s0", got.at[0])
    exchange("s1", sums.at[1], got.at[1], y, (d_up, d_dn, d_opp))
    zadd(3)
    third(2)
    hi = pl.ds(N1, N2)
    errb[hi, :] = errb[hi, :] - (unit(2, y, 0, N2)[...].astype(F32) + red[2].astype(F32) + reu[2].astype(F32))
    cp.arrived("last", rz, d_z)
    errb[hi, :] = errb[hi, :] - rz[...].astype(F32)
    third(0)
    lo = pl.ds(0, N1)
    errb[lo, :] = errb[lo, :] - (unit(0, y, 0, N1)[...].astype(F32) + red[0, lo].astype(F32) + reu[0, lo].astype(F32))
    attr[...] = total("s1", got.at[1])[0:1, :]
    with mark("drain"):
        assert len(cp.keys) == NRECV, len(cp.keys)
        cp.drain(0, lambda n: wdec.at[pl.ds(0, n)], 8192 * 2, d_z)
        cp.drain(4, lambda n: wdec.at[pl.ds(0, n)], 8192 * 2, d_z)
        cp.drain(1, lambda n: X.at[pl.ds(0, n), 0, 0], 65536, d_z)
        cp.drain(2, lambda n: acts, ROWS * FD * 2, d_z)
        cp.drain(3, lambda n: part.at[0, pl.ds(0, n)], 1024, d_z)


def write_out(fa, err, attr, fa_h, err_h, attr_h, sem):
    copies = [pltpu.make_async_copy(s, d, sem.at[i])
              for i, (s, d) in enumerate(((fa, fa_h), (err, err_h), (attr, attr_h)))]
    for copy in copies:
        copy.start()
    for copy in copies:
        copy.wait()


def per_device(resid, resid_grad, active, w_enc, b_enc, w_dec, b_dec):
    any_, vmem = pl.BlockSpec(memory_space=pl.ANY), pl.BlockSpec(memory_space=pltpu.VMEM)
    V = pltpu.VMEM
    outs = [((ROWS, FD), F32), ((ROWS, 512), F32), ((1, ROWS), F32)]
    held = pl.pallas_call(
        kernel,
        out_shape=tuple(V(*o) for o in outs),
        in_specs=[any_] * 7,
        out_specs=(vmem, vmem, vmem),
        scratch_shapes=[
            pltpu.SMEM(active.shape, active.dtype),
            V(b_enc.shape, F32),
            V(b_dec.shape, F32),
            V((8, 2, NX, 2, 64, ROWS), BF16),
            V((8, 2, NX, 2, 64, ROWS), BF16),
            V((NX, 2, 8, 128, FD), BF16),
            V((FD, 8192), BF16),
            V((8, FD, 512), BF16),
            V((ROWS, FD), F32),
            V((ROWS, FD), BF16),
            V((ROWS, FD), BF16),
            V((FD, ROWS), F32),
            V((8, ROWS, 512), BF16),
            V((NY, N1, 512), BF16),
            V((3, 80, 512), BF16),
            V((3, 80, 512), BF16),
            V((3, N2, 512), BF16),
            V((3, N2, 512), BF16),
            V((N2, 512), BF16),
            V((2, 8, ROWS), F32),
            V((2, 4, 8, ROWS), F32),
            pltpu.SemaphoreType.DMA((7,)),
            pltpu.SemaphoreType.DMA((5,)),
            pltpu.SemaphoreType.DMA((NRECV,)),
        ],
        compiler_params=pltpu.CompilerParams(
            collective_id=0, has_side_effects=True, vmem_limit_bytes=58 * 1024 * 1024),
    )(resid.T, resid_grad.T, active, w_enc.reshape(NX, 2, 8, 128, FD), b_enc, w_dec, b_dec)
    fa, err, attr = pl.pallas_call(
        write_out,
        out_shape=tuple(jax.ShapeDtypeStruct(*o) for o in outs),
        in_specs=[vmem] * 3,
        out_specs=(any_,) * 3,
        scratch_shapes=[pltpu.SemaphoreType.DMA((3,))],
    )(*(pltpu.with_memory_space_constraint(h, pltpu.VMEM) for h in held))
    return fa, err, attr.reshape(ROWS)


def solution(mesh):
    placed = (
        P(None, ("tok", "feat")),
        P(None, ("tok", "feat")),
        P("tok", None),
        P(None, "feat"),
        P("feat"),
        P("feat", None),
        P("feat"),
    )
    return jax.shard_map(
        per_device,
        mesh=mesh,
        in_specs=placed,
        out_specs=(P("tok", "feat"), P("tok", "feat"), P("tok")),
        check_vma=False,
    )
```
